32 devices in a mesh: section: 2 (over x), tile: 8 (over z, y), member: 2 (over core).
Axes of the slice: x: 2, y: 2, z: 4, core: 2. Of those that a mesh axis runs over, the one named last changes fastest.
Arguments:
- frames: bfloat16 [2, 16, 128, 8, 128], P(None, ('member', 'tile')), parts along dimension 1, may hold values from -6 to 6
- hidden_init: bfloat16 [4, 16, 128, 8, 128], P('section', ('member', 'tile')), parts along dimension 1, may hold values from -0.8984375 to 0.8984375
- memory_init: float32 [4, 16, 128, 8, 128], P('section', ('member', 'tile')), parts along dimension 1, may hold values from -4 to 4
- weights: bfloat16 [4, 512, 2304], P('section'), may hold values from -0.125 to 0.125
- biases: float32 [4, 512], P('section'), may hold values from -3 to 3
Outputs:
- hidden_out: bfloat16 [4, 16, 128, 8, 128], P('section', ('member', 'tile')), parts along dimension 1
- memory_out: float32 [4, 16, 128, 8, 128], P('section', ('member', 'tile')), parts along dimension 1
- gates_out: bfloat16 [2, 4, 16, 512, 8, 128], P(None, 'section', ('member', 'tile')), parts along dimension 2
The draws below stay inside these ranges and needn't reach their ends.
There are 2 independent parts, one for each index of `member`. The reference program is written for one: setup_inputs(seed, part) draws one part's arguments, and reference() takes and returns one part's arrays. A program takes and returns all parts, laid end to end along the dimension named above; an argument that names none is the same for every part. Nothing has to cross between parts.
All inputs are finite; a program needn't handle non-finite values.
Results may differ from the reference program's by a relative error of at most 0.0021.
Values may be sent and summed in bfloat16 or wider, within the bound.
No kernel may reach another device: no remote copies, remote signals or barrier semaphores. Data moves between devices by JAX's collectives and lax.ppermute only.
A program may use at most 128 MiB of HBM per device.

```python
import jax
import jax.numpy as jnp

HID = 128
TILE_ROWS = 8
TILE_COLS = 128
GRID_COLS = 8
STEPS = 2
TILES = 8
LAYERS = 4


def block_levels(rng, extent, pieces, smallest, top_value):
    def one(dim, blocks):
        steps = jax.random.uniform(jax.random.fold_in(jax.random.fold_in(rng, 6), dim), (blocks,), jnp.float32, smallest / len(pieces), top_value / len(pieces))
        return jnp.repeat(jnp.exp(steps), extent[dim] // blocks).reshape((-1,) + (1,) * (len(extent) - dim - 1))

    gain = one(*pieces[0])
    for cut in pieces[1:]:
        gain = gain * one(*cut)
    return gain


def scatter_about(rng, shape, deviation, bound, pieces=(), dtype=jnp.bfloat16):
    result = jax.random.normal(rng, shape, jnp.float32) * deviation
    if len(pieces) > 0:
        result = block_levels(rng, shape, pieces, -0.22, 0.18) * result
    return jnp.clip(result, min=-bound, max=bound).astype(dtype)


def setup_inputs(seed: int = 0, part: int = 0) -> dict:
    arg_keys = jax.random.split(jax.random.key(seed), 6)
    part_splits = jax.random.split(jax.random.fold_in(arg_keys[5], part), 6)
    return {
        "frames": scatter_about(part_splits[0], (STEPS, TILES, HID, TILE_ROWS, TILE_COLS), 1.0, 6.0, ((1, 8),)),
        "hidden_init": jnp.clip(jax.random.uniform(part_splits[1], (LAYERS, TILES, HID, TILE_ROWS, TILE_COLS), jnp.float32, -0.8984375, 0.8984375) * block_levels(part_splits[1], (LAYERS, TILES, HID, TILE_ROWS, TILE_COLS), ((0, 2), (1, 8)), -0.4, 0.0), -0.8984375, 0.8984375).astype(jnp.bfloat16),
        "memory_init": scatter_about(part_splits[2], (LAYERS, TILES, HID, TILE_ROWS, TILE_COLS), 1.0, 4.0, ((0, 2), (1, 8)), jnp.float32),
        "weights": scatter_about(arg_keys[3], (LAYERS, 4 * HID, 18 * HID), (18 * HID) ** -0.5, 0.125, ((0, 2),)),
        "biases": scatter_about(arg_keys[4], (LAYERS, 4 * HID), 0.5, 3.0, ((0, 2),), jnp.float32),
    }


def to_frame(tile_array):
    tile_count, depth_count, height, breadth = tile_array.shape
    grid_rows = tile_count // GRID_COLS
    placed = jnp.roll(tile_array, GRID_COLS + GRID_COLS // 2, axis=0)
    shaped = placed.reshape(grid_rows, GRID_COLS, depth_count, height, breadth)
    return shaped.transpose(2, 0, 3, 1, 4).reshape(depth_count, grid_rows * height, GRID_COLS * breadth)


def to_tiles(full_field):
    depth_count = full_field.shape[0]
    grid_rows = full_field.shape[1] // TILE_ROWS
    shaped = full_field.reshape(depth_count, grid_rows, TILE_ROWS, GRID_COLS, TILE_COLS)
    placed = shaped.transpose(1, 3, 0, 2, 4).reshape(grid_rows * GRID_COLS, depth_count, TILE_ROWS, TILE_COLS)
    return jnp.roll(placed, -(GRID_COLS + GRID_COLS // 2), axis=0)


def gate_inputs(stacked, layer_weights, bias_row):
    depth_count, height, breadth = stacked.shape
    padded = jnp.pad(stacked, ((0, 0), (1, 1), (1, 1)))
    running_total = jnp.zeros((layer_weights.shape[0], height * breadth), jnp.float32)
    for offset in range(9):
        row_offset = offset // 3
        column_offset = offset % 3
        window = padded[:, row_offset:row_offset + height, column_offset:column_offset + breadth].reshape(depth_count, height * breadth)
        kernel = layer_weights[:, offset * depth_count:(offset + 1) * depth_count]
        running_total = running_total + jnp.dot(kernel, window, preferred_element_type=jnp.float32)
    running_total = running_total + bias_row[:, None]
    return running_total.reshape(4, layer_weights.shape[0] // 4, height, breadth)


def reference(frames, hidden_init, memory_init, weights, biases):
    states = [to_frame(hidden_init[layer_index]) for layer_index in range(LAYERS)]
    memories = [to_frame(memory_init[layer_index]) for layer_index in range(LAYERS)]
    saved_gates = []
    for moment in range(STEPS):
        sources = [to_frame(frames[moment])] + states[:-1]
        fresh_states = []
        fresh_memories = []
        opened_step = []
        for layer_index in range(LAYERS):
            stacked = jnp.concatenate([sources[layer_index], states[layer_index]], axis=0)
            preact = gate_inputs(stacked, weights[layer_index], biases[layer_index])
            inflow = jax.nn.sigmoid(preact[0])
            forget = jax.nn.sigmoid(preact[1])
            outflow = jax.nn.sigmoid(preact[2])
            candidate = jnp.tanh(preact[3])
            memory = forget * memories[layer_index] + inflow * candidate
            hidden_state = (outflow * jnp.tanh(memory)).astype(jnp.bfloat16)
            opened = jnp.concatenate([inflow, forget, outflow, candidate], axis=0).astype(jnp.bfloat16)
            fresh_states.append(hidden_state)
            fresh_memories.append(memory)
            opened_step.append(to_tiles(opened))
        states = fresh_states
        memories = fresh_memories
        saved_gates.append(jnp.stack(opened_step))
    hidden_out = jnp.stack([to_tiles(item) for item in states])
    memory_out = jnp.stack([to_tiles(item) for item in memories])
    return (hidden_out, memory_out, jnp.stack(saved_gates))
```

```python
import jax
import jax.numpy as jnp
from jax import lax
from jax.experimental import pallas as pl
from jax.experimental.pallas import tpu as pltpu
from jax.sharding import PartitionSpec as P

GRID_COLS = 8
LANES = 128

bf16 = jnp.bfloat16
f32 = jnp.float32
VMEM = pl.BlockSpec(memory_space=pltpu.VMEM)
ANY = pl.BlockSpec(memory_space=pl.ANY)
EDGE = 16


def iota(shape, dim):
    return lax.broadcasted_iota(jnp.int32, shape, dim)


def params():
    return pltpu.CompilerParams(vmem_limit_bytes=24 * 2**20)


def in_vmem(array):
    return pltpu.with_memory_space_constraint(array, pltpu.VMEM)


def tile_place():
    return (lax.axis_index("tile") + GRID_COLS + GRID_COLS // 2) % lax.axis_size("tile")


def swap_pairs(parity):
    count = lax.axis_size("tile")
    index = {(k + GRID_COLS + GRID_COLS // 2) % count: k for k in range(count)}
    pairs = []
    for place in range(count - 1):
        if place % 2 == parity and place % GRID_COLS != GRID_COLS - 1:
            pairs += [(index[place], index[place + 1]), (index[place + 1], index[place])]
    return pairs


def swap_matrix(rows, block, to_rows_first):
    size = rows * block
    m = iota((size, size), 0)
    n = iota((size, size), 1)
    if to_rows_first:
        m, n = n, m
    return jnp.where((m // rows == n % block) & (m % rows == n // block), 1.0, 0.0).astype(bf16)


def prep_kernel(frames, hidden, memory, bias, xt, first_edges, second_edges, cells, wide_bias, raw, sems):
    layers, flat, _ = hidden.shape
    rows = xt.shape[0]
    channels = flat // rows
    copies = [
        pltpu.make_async_copy(hidden, raw.at[pl.ds(0, layers)], sems.at[0]),
        pltpu.make_async_copy(frames, raw.at[pl.ds(layers, frames.shape[0])], sems.at[1]),
        pltpu.make_async_copy(memory, cells, sems.at[2]),
    ]
    for copy in copies:
        copy.start()
    gates = wide_bias.shape[1]
    for layer in range(layers):
        for q in range(4):
            part = bias[layer : layer + 1, q * channels : (q + 1) * channels]
            part = jnp.broadcast_to(part, (channels, channels)).T
            wide_bias[layer, q * channels : (q + 1) * channels] = part * (0.5 if q < 3 else 1.0)
    block = 256 // rows
    order = swap_matrix(rows, block, True)
    count = raw.shape[0]
    width = rows * LANES
    m = iota((width, LANES), 0)
    lane = iota((width, LANES), 1)
    near = lane // rows
    to_right = (lane < 2 * rows) & (m == (lane % rows) * LANES + (LANES - 2) + near)
    to_left = (lane < 2 * rows) & (m == (lane % rows) * LANES + 1 - near)
    select = jnp.concatenate(
        [jnp.where(to_right, 1.0, 0.0).astype(bf16), jnp.where(to_left, 1.0, 0.0).astype(bf16)], axis=1
    )
    copies[0].wait()
    copies[1].wait()
    for pair in range(0, count, 2):
        for group in range(channels // block):
            part = pl.ds(group * 256, 256)
            both = jnp.concatenate([raw[pair, part], raw[pair + 1, part]], axis=1)
            out = jnp.dot(order, both, preferred_element_type=f32).astype(bf16)
            for r in range(rows):
                for k in range(2):
                    at = (pair + k) * channels + group * block
                    xt[r, at : at + block] = out[r * block : (r + 1) * block, k * LANES : (k + 1) * LANES]
    wide = jnp.concatenate([xt[r] for r in range(rows)], axis=1)
    edges = jnp.dot(wide, select, preferred_element_type=f32)
    right = jnp.zeros((channels, LANES), f32)
    left = jnp.zeros((channels, LANES), f32)
    for k in range(count):
        part = edges[k * channels : (k + 1) * channels]
        right += pltpu.roll(part[:, :LANES], k * EDGE, 1)
        left += pltpu.roll(part[:, LANES:], k * EDGE, 1)
    copies[2].wait()
    lane = iota((channels, LANES), 1)
    cell_right = jnp.zeros((channels, LANES), f32)
    cell_left = jnp.zeros((channels, LANES), f32)
    for layer in range(layers):
        for r in range(rows):
            row = cells[layer, pl.ds(r, channels, stride=rows), :]
            to = (count + layer) * EDGE + r
            cell_right = jnp.where(lane == to, pltpu.roll(row, (to + 1) % LANES, 1), cell_right)
            cell_left = jnp.where(lane == to, pltpu.roll(row, to, 1), cell_left)

    def split(value):
        high = value.astype(bf16)
        low = (value - high.astype(f32)).astype(bf16)
        return high.astype(f32) + pltpu.roll(low.astype(f32), rows, 1)

    right = (right + split(cell_right)).astype(bf16)
    left = (left + split(cell_left)).astype(bf16)
    even = tile_place() % 2 == 0
    first_edges[...] = jnp.where(even, right, left)
    second_edges[...] = jnp.where(even, left, right)


def pick(lane, start, size, value, rest):
    return jnp.where((lane >= start) & (lane < start + size), value, rest)


def edge_kernel(xt, first_own, second_own, first_got, second_got, packet, packed, next_edge, cell_edge):
    rows = xt.shape[0]
    channels = packet.shape[1]
    layers = cell_edge.shape[0]
    even = tile_place() % 2 == 0
    own_right = jnp.where(even, first_own[...], second_own[...]).astype(f32)
    own_left = jnp.where(even, second_own[...], first_own[...]).astype(f32)
    from_left = jnp.where(even, second_got[...], first_got[...]).astype(f32)
    from_right = jnp.where(even, first_got[...], second_got[...]).astype(f32)
    lane = iota((channels, LANES), 1)

    def turned(value, by):
        return pltpu.roll(value, by % LANES, 1)

    def columns(k):
        base = -k * EDGE
        out = jnp.zeros((channels, LANES), f32)
        out = pick(lane, 0, rows, turned(from_left, base), out)
        out = pick(lane, rows, rows, turned(own_right, base), out)
        out = pick(lane, 2 * rows, rows, turned(from_left, base + rows), out)
        out = pick(lane, 3 * rows, rows, turned(from_right, base + 2 * rows), out)
        out = pick(lane, 4 * rows, rows, turned(own_left, base + 3 * rows), out)
        out = pick(lane, 5 * rows, rows, turned(from_right, base + 5 * rows), out)
        return out.astype(bf16)

    last = layers - 1
    for k in range(layers + 1):
        packed[k] = columns(k)
    next_edge[...] = columns(layers + 1)
    packet[rows] = packed[last]
    for r in range(rows):
        packet[r] = xt[r, last * channels : (last + 1) * channels]
    for layer in range(layers):
        base = -(layers + 2 + layer) * EDGE
        a = turned(from_left, base)
        b = turned(from_right, base)
        a = a + turned(a, -rows)
        b = b + turned(b, -rows)
        cell_edge[layer] = jnp.where(lane < rows, a, turned(b, rows))


def cell_step(pre, bias, memory):
    channels = memory.shape[0]

    def gate(q):
        part = slice(q * channels, (q + 1) * channels)
        if q == 3:
            return jnp.tanh(pre[part] + bias[part])
        return jnp.tanh(pre[part] * 0.5 + bias[part]) * 0.5 + 0.5

    inflow, forget, outflow, candidate = gate(0), gate(1), gate(2), gate(3)
    memory = forget * memory + inflow * candidate
    hidden = (outflow * jnp.tanh(memory)).astype(bf16)
    return (inflow, forget, outflow, candidate), memory, hidden


def run_layer(sources, edge_columns, weights, bias, memory_of, memory_out, hidden_rows, cell_edge, gates_at, scratch):
    shifted, gate_rows, gate_tiles, sems = scratch
    rows = shifted.shape[1] - 2
    channels = shifted.shape[2] // 2
    lane = iota((channels, LANES), 1)
    blank = jnp.zeros((2 * channels, LANES), bf16)
    for b in range(3):
        shifted[b, 0] = blank
        shifted[b, rows + 1] = blank
    for k in range(2):
        part = slice(k * channels, (k + 1) * channels)
        for r in range(rows):
            x = sources[k](r)
            before = pltpu.roll(edge_columns[k], LANES - 2 * rows - r, 1)
            after = pltpu.roll(edge_columns[k], LANES - 1 - 3 * rows - r, 1)
            shifted[1, r + 1, part] = x
            shifted[0, r + 1, part] = jnp.where(lane == 0, before, pltpu.roll(x, 1, 1))
            shifted[2, r + 1, part] = jnp.where(lane == LANES - 1, after, pltpu.roll(x, LANES - 1, 1))
    for j in range(rows // 2):
        patches = jnp.concatenate(
            [
                jnp.concatenate([shifted[b, 2 * j + a], shifted[b, 2 * j + a + 1]], axis=1)
                for a in range(3)
                for b in range(3)
            ],
            axis=0,
        )
        total = jnp.dot(weights, patches, preferred_element_type=f32)
        for k in range(2):
            r = 2 * j + k
            at = pl.ds(r, channels, stride=rows)
            gates, memory, hidden = cell_step(total[:, k * LANES : (k + 1) * LANES], bias, memory_of(at))
            memory_out[at, :] = memory
            hidden_rows[r] = hidden
            for q in range(4):
                gate_rows[r, q * channels : (q + 1) * channels] = gates[q].astype(bf16)
    if cell_edge is not None:
        wide = jnp.concatenate(edge_columns, axis=0)
        wide_lane = iota((2 * channels, LANES), 1)
        parts = []
        for a in range(3):
            row = wide_lane % rows + (a - 1)
            for b in range(3):
                moved = pltpu.roll(wide, (-2 * rows * b - (a - 1)) % LANES, 1)
                parts.append(jnp.where((row >= 0) & (row < rows), moved, jnp.zeros_like(moved)))
        total = jnp.dot(weights, jnp.concatenate(parts, axis=0), preferred_element_type=f32)
        _, _, hidden = cell_step(total, bias, cell_edge)
        place = tile_place() % GRID_COLS
        inside = ((lane < rows) & (place > 0)) | ((lane >= rows) & (lane < 2 * rows) & (place < GRID_COLS - 1))
        hidden = jnp.where(inside, hidden, jnp.zeros_like(hidden))
        hidden_rows[rows] = pltpu.roll(hidden, 2 * rows, 1)
    copies = []
    for first in range(0, gate_rows.shape[1] * rows, 512):
        restore(gate_rows, gate_tiles, first)
        part = pl.ds(first, 512)
        copy = pltpu.make_async_copy(gate_tiles.at[part], gates_at.at[part], sems.at[first // 512])
        copy.start()
        copies.append(copy)
    return copies


def restore(source, target, first):
    rows = source.shape[0]
    block = 256 // rows
    order = swap_matrix(rows, block, False)
    both = []
    for at in (first // rows, first // rows + block):
        both.append(jnp.concatenate([source[r, at : at + block] for r in range(rows)], axis=0))
    out = jnp.dot(order, jnp.concatenate(both, axis=1), preferred_element_type=f32).astype(bf16)
    target[first : first + 256] = out[:, :LANES]
    target[first + 256 : first + 512] = out[:, LANES:]


def finish(copies):
    for copy in copies:
        copy.wait()


def part_of(ref, k, channels):
    def load(r):
        return ref[r, k * channels : (k + 1) * channels]

    return load


def either(condition, one, other):
    def load(r):
        return jnp.where(condition, one(r), other(r))

    return load


def whole(ref):
    return lambda r: ref[r]


def first_last_layer(xt, packed, weights, bias, cells, cell_edge, hidden, memory, gates, *scratch):
    layer = weights.shape[0] - 1
    copies = run_layer(
        (part_of(xt, layer - 1, packed.shape[1]), part_of(xt, layer, packed.shape[1])),
        (packed[layer - 1], packed[layer]),
        weights[layer],
        bias[layer],
        lambda at: cells[layer, at, :],
        memory,
        hidden,
        cell_edge[layer],
        gates.at[0, layer],
        scratch,
    )
    finish(copies)


def first_first_layer(
    xt, packet, packed, weights, bias, cells, cell_edge, _, hidden, memory, gates, *scratch
):
    first = lax.axis_index("section") == 0
    layers = weights.shape[0]
    rows = packet.shape[0] - 1
    copies = run_layer(
        (either(first, part_of(xt, layers, packet.shape[1]), whole(packet)), part_of(xt, 0, packet.shape[1])),
        (jnp.where(first, packed[layers], packet[rows]), packed[0]),
        weights[0],
        bias[0],
        lambda at: cells[0, at, :],
        memory,
        hidden,
        cell_edge[0],
        gates.at[0, 0],
        scratch,
    )
    finish(copies)


def close_layer(layer, scratch, hidden_rows, hidden_tiles, memory_tiles, hidden_out, memory_out, sems):
    flat = hidden_tiles.shape[0]
    saves = [pltpu.make_async_copy(memory_tiles, memory_out.at[layer], sems.at[0])]
    saves[0].start()
    for first in range(0, flat, 512):
        restore(hidden_rows, hidden_tiles, first)
    saves.append(pltpu.make_async_copy(hidden_tiles, hidden_out.at[layer], sems.at[1]))
    saves[1].start()
    return saves


def second_last_layer(before, last, weights, bias, memory, _, gates, hidden_out, memory_out, *scratch):
    *scratch, hidden_rows, hidden_tiles, memory_tiles, sems = scratch
    layer = weights.shape[0] - 1
    rows = before.shape[0] - 1
    copies = run_layer(
        (whole(before), whole(last)),
        (before[rows], last[rows]),
        weights[layer],
        bias[layer],
        lambda at: memory[at, :],
        memory_tiles,
        hidden_rows,
        None,
        gates.at[1, layer],
        scratch,
    )
    copies += close_layer(
        layer, scratch, hidden_rows, hidden_tiles, memory_tiles, hidden_out, memory_out, sems
    )
    finish(copies)


def second_first_layer(
    xt, packet, next_edge, last, weights, bias, memory, _, __, ___, gates, hidden_out, memory_out, *scratch
):
    *scratch, hidden_rows, hidden_tiles, memory_tiles, sems = scratch
    first = lax.axis_index("section") == 0
    rows = packet.shape[0] - 1
    frame = xt.shape[1] // packet.shape[1] - 1
    copies = run_layer(
        (either(first, part_of(xt, frame, packet.shape[1]), whole(packet)), whole(last)),
        (jnp.where(first, next_edge[...], packet[rows]), last[rows]),
        weights[0],
        bias[0],
        lambda at: memory[at, :],
        memory_tiles,
        hidden_rows,
        None,
        gates.at[1, 0],
        scratch,
    )
    copies += close_layer(
        0, scratch, hidden_rows, hidden_tiles, memory_tiles, hidden_out, memory_out, sems
    )
    finish(copies)


def wavefront(frames, hidden_init, memory_init, weights, biases):
    steps, _, channels, rows, _ = frames.shape
    layers, gate_count, _ = weights.shape
    flat = channels * rows
    frames = frames.reshape(steps, flat, LANES)
    hidden_init = hidden_init.reshape(layers, flat, LANES)
    memory_init = memory_init.reshape(layers, flat, LANES)
    plane = (channels, LANES)
    sections = lax.axis_size("section")
    ahead = [(i, i + 1) for i in range(sections - 1)]

    def call(kernel, ins, outs, scratch=(), aliases=None, places=None):
        return pl.pallas_call(
            kernel,
            in_specs=places[0] if places else [VMEM] * len(ins),
            out_specs=places[1] if places else [VMEM] * len(outs),
            out_shape=outs,
            scratch_shapes=list(scratch),
            input_output_aliases=aliases or {},
            compiler_params=params(),
        )(*ins)

    xt, first_edges, second_edges, cells, wide_bias = call(
        prep_kernel,
        (frames, hidden_init, memory_init, biases),
        [
            pltpu.VMEM((rows, (layers + steps) * channels, LANES), bf16),
            pltpu.VMEM(plane, bf16),
            pltpu.VMEM(plane, bf16),
            pltpu.VMEM((layers, flat, LANES), f32),
            pltpu.VMEM((layers, gate_count, LANES), f32),
        ],
        [pltpu.VMEM((layers + steps, flat, LANES), bf16), pltpu.SemaphoreType.DMA((3,))],
        places=([ANY, ANY, ANY, VMEM], [VMEM] * 5),
    )
    first_got = in_vmem(lax.ppermute(first_edges, "tile", swap_pairs(0)))
    second_got = in_vmem(lax.ppermute(second_edges, "tile", swap_pairs(1)))
    packet, packed, next_edge, cell_edge = call(
        edge_kernel,
        (xt, first_edges, second_edges, first_got, second_got),
        [
            pltpu.VMEM((rows + 1,) + plane, bf16),
            pltpu.VMEM((layers + 1,) + plane, bf16),
            pltpu.VMEM(plane, bf16),
            pltpu.VMEM((layers,) + plane, f32),
        ],
    )
    packet = in_vmem(lax.ppermute(packet, "section", ahead))
    work = [
        pltpu.VMEM((3, rows + 2, 2 * channels, LANES), bf16),
        pltpu.VMEM((rows, gate_count, LANES), bf16),
        pltpu.VMEM((gate_count * rows, LANES), bf16),
        pltpu.SemaphoreType.DMA((gate_count * rows // 512,)),
    ]
    gates_shape = jax.ShapeDtypeStruct((steps, layers, gate_count * rows, LANES), bf16)
    fresh = [pltpu.VMEM((rows + 1,) + plane, bf16), pltpu.VMEM((flat, LANES), f32), gates_shape]
    last, last_memory, gates = call(
        first_last_layer,
        (xt, packed, weights, wide_bias, cells, cell_edge),
        fresh,
        work,
        places=([VMEM] * 6, [VMEM, VMEM, ANY]),
    )
    next_packet = in_vmem(lax.ppermute(last, "section", ahead))
    before, before_memory, gates = call(
        first_first_layer,
        (xt, packet, packed, weights, wide_bias, cells, cell_edge, gates),
        fresh,
        work,
        aliases={7: 2},
        places=([VMEM] * 7 + [ANY], [VMEM, VMEM, ANY]),
    )
    final = [
        gates_shape,
        jax.ShapeDtypeStruct((layers, flat, LANES), bf16),
        jax.ShapeDtypeStruct((layers, flat, LANES), f32),
    ]
    close = work + [
        pltpu.VMEM((rows,) + plane, bf16),
        pltpu.VMEM((flat, LANES), bf16),
        pltpu.VMEM((flat, LANES), f32),
        pltpu.SemaphoreType.DMA((2,)),
    ]
    gates, hidden_out, memory_out = call(
        second_last_layer,
        (before, last, weights, wide_bias, last_memory, gates),
        final,
        close,
        aliases={5: 0},
        places=([VMEM] * 5 + [ANY], [ANY] * 3),
    )
    gates, hidden_out, memory_out = call(
        second_first_layer,
        (xt, next_packet, next_edge, before, weights, wide_bias, before_memory, gates, hidden_out, memory_out),
        final,
        close,
        aliases={7: 0, 8: 1, 9: 2},
        places=([VMEM] * 7 + [ANY] * 3, [ANY] * 3),
    )
    return (
        hidden_out.reshape(layers, 1, channels, rows, LANES),
        memory_out.reshape(layers, 1, channels, rows, LANES),
        gates.reshape(steps, layers, 1, gate_count, rows, LANES),
    )


def from_behind(block, axis, distance):
    devices = range(lax.axis_size(axis))
    route = [((i - distance) % len(devices), i) for i in devices]
    return lax.ppermute(block, axis, route)


def shifted(shard, axis, by):
    peers = lax.axis_size(axis)
    pairs = [(i, i + by) for i in range(peers) if 0 <= i + by < peers]
    return lax.ppermute(shard, axis, pairs)


def keep_if(condition, rim):
    return jnp.where(condition, rim, jnp.zeros_like(rim))


def with_rims(source_field):
    place = tile_place()
    row_place, column_place = (place // GRID_COLS, place % GRID_COLS)
    grid_rows = lax.axis_size("tile") // GRID_COLS
    upper_rim = from_behind(source_field[:, -1:, :], "tile", GRID_COLS)
    lower_rim = from_behind(source_field[:, :1, :], "tile", -GRID_COLS)
    upper_rim = keep_if(row_place > 0, upper_rim)
    lower_rim = keep_if(row_place < grid_rows - 1, lower_rim)
    heightened = jnp.concatenate([upper_rim, source_field, lower_rim], axis=1)
    left_rim = from_behind(heightened[:, :, -1:], "tile", 1)
    right_rim = from_behind(heightened[:, :, :1], "tile", -1)
    left_rim = keep_if(column_place > 0, left_rim)
    right_rim = keep_if(column_place < GRID_COLS - 1, right_rim)
    return jnp.concatenate([left_rim, heightened, right_rim], axis=2)


def hand_over(hidden_state):
    return shifted(hidden_state, "section", 1)


def advance(stacked, layer_weights, bias_row, memory):
    hidden_count = memory.shape[0]
    height = stacked.shape[1] - 2
    breadth = stacked.shape[2] - 2
    shifted_views = [
        stacked[:, row_offset : row_offset + height, column_offset : column_offset + breadth]
        for row_offset in range(3)
        for column_offset in range(3)
    ]
    patches = jnp.concatenate(shifted_views, axis=0).reshape(9 * stacked.shape[0], height * breadth)
    preact = jnp.dot(layer_weights, patches, preferred_element_type=jnp.float32) + bias_row[:, None]
    preact = preact.reshape(4, hidden_count, height, breadth)
    inflow = jax.nn.sigmoid(preact[0])
    forget = jax.nn.sigmoid(preact[1])
    outflow = jax.nn.sigmoid(preact[2])
    candidate = jnp.tanh(preact[3])
    memory = forget * memory + inflow * candidate
    hidden_state = (outflow * jnp.tanh(memory)).astype(jnp.bfloat16)
    opened = (
        jnp.stack([inflow, forget, outflow, candidate])
        .reshape(4 * hidden_count, height, breadth)
        .astype(jnp.bfloat16)
    )
    return (hidden_state, memory, opened)


def general_body(frames, hidden_init, memory_init, weights, biases):
    step_count = frames.shape[0]
    layer_count = weights.shape[0]
    channels = frames.shape[2]
    first_section = lax.axis_index("section") == 0
    saved_gates = []
    states = [hidden_init[layer_index, 0] for layer_index in range(layer_count)]
    memories = [memory_init[layer_index, 0] for layer_index in range(layer_count)]
    for moment in range(step_count):
        received = hand_over(states[-1])
        incoming = jnp.where(first_section, frames[moment, 0], received)
        padded = with_rims(jnp.concatenate([incoming] + states, axis=0))
        layer_stacks = [
            padded[layer_index * channels : (layer_index + 2) * channels]
            for layer_index in range(layer_count)
        ]
        fresh_states = []
        fresh_memories = []
        opened_step = []
        for layer_index in range(layer_count):
            hidden_state, memory, opened = advance(
                layer_stacks[layer_index],
                weights[layer_index],
                biases[layer_index],
                memories[layer_index],
            )
            fresh_states.append(hidden_state)
            fresh_memories.append(memory)
            opened_step.append(opened)
        states = fresh_states
        memories = fresh_memories
        saved_gates.append(jnp.stack(opened_step))
    hidden_out = jnp.stack(states)[:, None]
    memory_out = jnp.stack(memories)[:, None]
    gates_out = jnp.stack(saved_gates)[:, :, None]
    return (hidden_out, memory_out, gates_out)


def body(frames, hidden_init, memory_init, weights, biases):
    one_row = lax.axis_size("tile") == GRID_COLS
    if one_row and frames.shape[0] == 2 and weights.shape[0] == 2:
        return wavefront(frames, hidden_init, memory_init, weights, biases)
    return general_body(frames, hidden_init, memory_init, weights, biases)


def solution(mesh):
    in_specs = (
        P(None, ("member", "tile"), None, None, None),
        P("section", ("member", "tile"), None, None, None),
        P("section", ("member", "tile"), None, None, None),
        P("section", None, None),
        P("section", None),
    )
    out_specs = (
        P("section", ("member", "tile"), None, None, None),
        P("section", ("member", "tile"), None, None, None),
        P(None, "section", ("member", "tile"), None, None, None),
    )
    return jax.shard_map(body, mesh=mesh, in_specs=in_specs, out_specs=out_specs, check_vma=False)
```

```python
import functools

import jax
import jax.numpy as jnp
from jax import lax
from jax.experimental import pallas as pl
from jax.experimental.pallas import tpu as pltpu
from jax.sharding import PartitionSpec as P


GRID_COLS = 8
LANES = 128

bf16 = jnp.bfloat16
f32 = jnp.float32
VMEM = pl.BlockSpec(memory_space=pltpu.VMEM)
HBM = pl.BlockSpec(memory_space=pltpu.HBM)


def iota(shape, dim):
    return lax.broadcasted_iota(jnp.int32, shape, dim)


def params():
    return pltpu.CompilerParams(vmem_limit_bytes=24 * 2**20)


def in_vmem(array):
    return pltpu.with_memory_space_constraint(array, pltpu.VMEM)


def in_hbm(array):
    return pltpu.with_memory_space_constraint(array, pltpu.HBM)


def permuted(array, axis, pairs):
    return in_vmem(lax.ppermute(array, axis, pairs))


def tile_place():
    return (lax.axis_index("tile") + GRID_COLS + GRID_COLS // 2) % lax.axis_size("tile")


def swap_pairs(parity):
    count = lax.axis_size("tile")
    index = {(k + GRID_COLS + GRID_COLS // 2) % count: k for k in range(count)}
    pairs = []
    for place in range(count - 1):
        if place % 2 == parity and place % GRID_COLS != GRID_COLS - 1:
            pairs += [(index[place], index[place + 1]), (index[place + 1], index[place])]
    return pairs


def swap_matrix(rows, block, to_rows_first):
    size = rows * block
    m = iota((size, size), 0)
    n = iota((size, size), 1)
    if to_rows_first:
        m, n = n, m
    return jnp.where((m // rows == n % block) & (m % rows == n // block), 1.0, 0.0).astype(bf16)


def turned(value, by):
    return pltpu.roll(value, by % LANES, 1)


def prep_kernel(
    frames, hidden, memory, bias, weights, xt, sent, first_edges, second_edges, cells, wide_bias, last_weights,
    raw, raw_bias, sems,
):
    layers, _, _ = hidden.shape
    rows, channels, _ = sent.shape
    copies = [
        pltpu.make_async_copy(hidden, raw.at[pl.ds(0, layers)], sems.at[0]),
        pltpu.make_async_copy(frames, raw.at[pl.ds(layers, frames.shape[0])], sems.at[1]),
        pltpu.make_async_copy(memory, cells, sems.at[2]),
        pltpu.make_async_copy(bias, raw_bias, sems.at[3]),
        pltpu.make_async_copy(weights.at[layers - 1], last_weights, sems.at[4]),
    ]
    for copy in copies:
        copy.start()
    block = 256 // rows
    order = swap_matrix(rows, block, True)
    count = raw.shape[0]
    width = rows * LANES
    m = iota((width, LANES), 0)
    lane = iota((width, LANES), 1)
    near = lane // rows
    to_right = (lane < 2 * rows) & (m == (lane % rows) * LANES + (LANES - 2) + near)
    to_left = (lane < 2 * rows) & (m == (lane % rows) * LANES + 1 - near)
    select = jnp.concatenate(
        [jnp.where(to_right, 1.0, 0.0).astype(bf16), jnp.where(to_left, 1.0, 0.0).astype(bf16)], axis=1
    )
    for pair in range(0, count, 2):
        copies[pair // layers].wait()
        for group in range(channels // block):
            part = pl.ds(group * 256, 256)
            both = jnp.concatenate([raw[pair, part], raw[pair + 1, part]], axis=1)
            out = jnp.dot(order, both, preferred_element_type=f32).astype(bf16)
            for r in range(rows):
                for k in range(2):
                    piece = out[r * block : (r + 1) * block, k * LANES : (k + 1) * LANES]
                    at = (pair + k) * channels + group * block
                    xt[r, at : at + block] = piece
                    if pair + k == layers - 1:
                        sent[r, group * block : (group + 1) * block] = piece
    edge = 2 * rows
    lane = iota((channels, LANES), 1)
    cell_right = jnp.zeros((channels, LANES), f32)
    cell_left = jnp.zeros((channels, LANES), f32)
    copies[2].wait()
    for layer in range(layers):
        for r in range(rows):
            row = cells[layer, pl.ds(r, channels, stride=rows), :]
            to = (count + layer) * edge + r
            cell_right = jnp.where(lane == to, turned(row, to + 1), cell_right)
            cell_left = jnp.where(lane == to, turned(row, to), cell_left)
    wide = jnp.concatenate([xt[r] for r in range(rows)], axis=1)
    edges = jnp.dot(wide, select, preferred_element_type=f32)

    def split(value):
        high = value.astype(bf16)
        low = (value - high.astype(f32)).astype(bf16)
        return high.astype(f32) + turned(low.astype(f32), rows)

    right, left = split(cell_right), split(cell_left)
    for k in range(count):
        part = edges[k * channels : (k + 1) * channels]
        right += turned(part[:, :LANES], k * edge)
        left += turned(part[:, LANES:], k * edge)
    even = tile_place() % 2 == 0
    first_edges[...] = jnp.where(even, right, left).astype(bf16)
    second_edges[...] = jnp.where(even, left, right).astype(bf16)
    copies[3].wait()
    for layer in range(layers):
        for q in range(4):
            part = raw_bias[layer : layer + 1, q * channels : (q + 1) * channels]
            part = jnp.broadcast_to(part, (channels, channels)).T
            wide_bias[layer, q * channels : (q + 1) * channels] = part * (0.5 if q < 3 else 1.0)
    copies[4].wait()


def cell_step(pre, bias, memory):
    channels = memory.shape[0]

    def gate(q):
        part = slice(q * channels, (q + 1) * channels)
        if q == 3:
            return jnp.tanh(pre[part] + bias[part])
        return jnp.tanh(pre[part] * 0.5 + bias[part]) * 0.5 + 0.5

    inflow, forget, outflow, candidate = gate(0), gate(1), gate(2), gate(3)
    memory = forget * memory + inflow * candidate
    hidden = (outflow * jnp.tanh(memory)).astype(bf16)
    return (inflow, forget, outflow, candidate), memory, hidden


def run_layer(sources, edge_columns, weights, bias, memory_of, memory_out, hidden_rows, gate_rows, shifted, beside=()):
    rows = shifted.shape[1] - 2
    channels = shifted.shape[2] // 2
    lane = iota((channels, LANES), 1)
    blank = jnp.zeros((2 * channels, LANES), bf16)
    for b in range(3):
        shifted[b, 0] = blank
        shifted[b, rows + 1] = blank

    def build(r):
        for k in range(2):
            part = slice(k * channels, (k + 1) * channels)
            x = sources[k](r)
            if edge_columns is None:
                before = after = jnp.zeros_like(x)
            else:
                before = turned(edge_columns[k], -2 * rows - r)
                after = turned(edge_columns[k], -1 - 3 * rows - r)
            shifted[1, r + 1, part] = x
            shifted[0, r + 1, part] = jnp.where(lane == 0, before, turned(x, 1))
            shifted[2, r + 1, part] = jnp.where(lane == LANES - 1, after, turned(x, -1))

    beside = list(beside)
    tiles = rows // 2
    share = -(-len(beside) // tiles)
    for r in range(min(3, rows)):
        build(r)
    for j in range(tiles):
        patches = jnp.concatenate(
            [
                jnp.concatenate([shifted[b, 2 * j + a], shifted[b, 2 * j + a + 1]], axis=1)
                for a in range(3)
                for b in range(3)
            ],
            axis=0,
        )
        total = jnp.dot(weights, patches, preferred_element_type=f32)
        for r in (2 * j + 3, 2 * j + 4):
            if r < rows:
                build(r)
        for work in beside[j * share : (j + 1) * share]:
            work()
        for k in range(2):
            r = 2 * j + k
            at = pl.ds(r, channels, stride=rows)
            gates, memory, hidden = cell_step(total[:, k * LANES : (k + 1) * LANES], bias, memory_of(at))
            memory_out[at, :] = memory
            hidden_rows[r] = hidden
            for q in range(4):
                gate_rows[r, q * channels : (q + 1) * channels] = gates[q].astype(bf16)


def edge_step(columns, weights, bias, memory, rows):
    channels = memory.shape[0]
    lane = iota((2 * channels, LANES), 1)
    parts = []
    for a in range(3):
        row = lane % rows + (a - 1)
        for b in range(3):
            moved = turned(columns[b], 1 - a)
            parts.append(jnp.where((row >= 0) & (row < rows), moved, jnp.zeros_like(moved)))
    total = jnp.dot(weights, jnp.concatenate(parts, axis=0), preferred_element_type=f32)
    return cell_step(total, bias, memory)


def outer_columns(hidden, rows):
    lane = iota(hidden.shape, 1)
    place = tile_place() % GRID_COLS
    inside = ((lane < rows) & (place > 0)) | ((lane >= rows) & (lane < 2 * rows) & (place < GRID_COLS - 1))
    return turned(jnp.where(inside, hidden, jnp.zeros_like(hidden)), 2 * rows)


def restore(source, target, first):
    rows = source.shape[0]
    block = 256 // rows
    order = swap_matrix(rows, block, False)
    both = []
    for at in (first // rows, first // rows + block):
        both.append(jnp.concatenate([source[r, at : at + block] for r in range(rows)], axis=0))
    out = jnp.dot(order, jnp.concatenate(both, axis=1), preferred_element_type=f32).astype(bf16)
    target[first : first + 256] = out[:, :LANES]
    target[first + 256 : first + 512] = out[:, LANES:]


def saves(source, tiles, out, sems, started):
    def piece(first):
        def work():
            restore(source, tiles, first)
            part = pl.ds(first, 512)
            copy = pltpu.make_async_copy(tiles.at[part], out.at[part], sems.at[first // 512])
            copy.start()
            started.append(copy)

        return work

    return [piece(first) for first in range(0, tiles.shape[0], 512)]


def part_of(ref, k, channels):
    def load(r):
        return ref[r, k * channels : (k + 1) * channels]

    return load


def either(condition, one, other):
    def load(r):
        return jnp.where(condition, one(r), other(r))

    return load


def whole(ref):
    return lambda r: ref[r]


def first_last_layer(xt, last_weights, bias, cells, weights, gate_rows, memory, hidden, first_weights, shifted, sem):
    layer = bias.shape[0] - 1
    channels = hidden.shape[1]
    copy = pltpu.make_async_copy(weights.at[0], first_weights, sem)
    copy.start()
    run_layer(
        (part_of(xt, layer - 1, channels), part_of(xt, layer, channels)),
        None,
        last_weights[...],
        bias[layer],
        lambda at: cells[layer, at, :],
        memory,
        hidden,
        gate_rows,
        shifted,
    )
    copy.wait()


def pack_kernel(rows, first_own, second_own, first_got, second_got, packed, sent, next_edge, taps, cell_edge):
    channels = sent.shape[0]
    layers = cell_edge.shape[0]
    layer = layers - 1
    edge = 2 * rows
    even = tile_place() % 2 == 0
    own_right = jnp.where(even, first_own[...], second_own[...])
    own_left = jnp.where(even, second_own[...], first_own[...])
    from_left = jnp.where(even, second_got[...], first_got[...])
    from_right = jnp.where(even, first_got[...], second_got[...])
    lane = iota((channels, LANES), 1)

    def laid(k, pieces):
        out = jnp.zeros((channels, LANES), bf16)
        for slot, (value, block) in enumerate(pieces):
            value = turned(value, (slot - block) * rows - k * edge)
            out = jnp.where((lane >= slot * rows) & (lane < (slot + 1) * rows), value, out)
        return out

    outer = [(from_left, 0), (own_right, 1), (from_left, 1), (from_right, 1), (own_left, 1), (from_right, 0)]
    for k in range(layers + 1):
        packed[k] = laid(k, outer)
    sent[...] = packed[layer]
    next_edge[...] = laid(layers + 1, outer)
    inner = [
        [(from_left, 0), (own_right, 1), (from_left, 1), (own_right, 0)],
        [(from_left, 1), (from_right, 1), (own_left, 1), (own_right, 1)],
        [(own_left, 1), (from_right, 0), (own_left, 0), (from_right, 1)],
    ]
    for b in range(3):
        for k in range(2):
            taps[b, k * channels : (k + 1) * channels] = laid(layer - 1 + k, inner[b])
    for k in range(layers):
        high, low = (
            laid(layers + 2 + k, [(value, part) for value in (from_left, from_right, own_left, own_right)])
            for part in range(2)
        )
        cell_edge[k] = high.astype(f32) + low.astype(f32)


def mend_kernel(taps, last_weights, bias, cell_edge, gate_rows, memory, hidden, last, new_memory, new_gates):
    rows, channels, _ = hidden.shape
    layer = bias.shape[0] - 1
    gates, edge_memory, edge_hidden = edge_step(
        [taps[b] for b in range(3)], last_weights[...], bias[layer], cell_edge[layer], rows
    )
    last[rows] = outer_columns(edge_hidden, rows)
    gates = jnp.concatenate([gate.astype(bf16) for gate in gates], axis=0)

    def mended(value, column, r):
        lane = iota(value.shape, 1)
        value = jnp.where(lane == 0, turned(column, -2 * rows - r), value)
        return jnp.where(lane == LANES - 1, turned(column, -1 - 3 * rows - r), value)

    for r in range(rows):
        last[r] = mended(hidden[r], edge_hidden, r)
    for r in range(rows):
        at = pl.ds(r, channels, stride=rows)
        new_memory[at, :] = mended(memory[at, :], edge_memory, r)
        new_gates[r] = mended(gate_rows[r], gates, r)


def middle_kernel(
    xt, packet, packet_edge, packed, first_weights, last_weights, bias, cells, cell_edge, gate_rows, last, last_memory,
    before, before_memory, next_gates, next_memory, next_hidden, gates,
    shifted, first_gates, tiles, other_tiles, sems,
):
    first = lax.axis_index("section") == 0
    rows, channels, _ = packet.shape
    layers = bias.shape[0]
    started = []
    edges = (jnp.where(first, packed[layers], packet_edge[...]), packed[0])
    run_layer(
        (either(first, part_of(xt, layers, channels), whole(packet)), part_of(xt, 0, channels)),
        edges,
        first_weights[...],
        bias[0],
        lambda at: cells[0, at, :],
        before_memory,
        before,
        first_gates,
        shifted,
        saves(gate_rows, tiles, gates.at[0, layers - 1], sems.at[0], started),
    )
    wide = jnp.concatenate(edges, axis=0)
    columns = [turned(wide, -2 * rows * b) for b in range(3)]
    _, _, hidden = edge_step(columns, first_weights[...], bias[0], cell_edge[0], rows)
    before[rows] = outer_columns(hidden, rows)
    run_layer(
        (whole(before), whole(last)),
        (before[rows], last[rows]),
        last_weights[...],
        bias[layers - 1],
        lambda at: last_memory[at, :],
        next_memory,
        next_hidden,
        next_gates,
        shifted,
        saves(first_gates, other_tiles, gates.at[0, 0], sems.at[1], started),
    )
    for copy in started:
        copy.wait()


def final_kernel(
    xt, packet, next_edge, before, first_weights, bias, before_memory, last_gates, last_memory, last_hidden, _,
    gates, hidden_out, memory_out,
    shifted, first_gates, tiles, other_tiles, first_hidden, first_memory, hidden_tiles, other_hidden, sems, cell_sems,
):
    first = lax.axis_index("section") == 0
    rows = packet.shape[0] - 1
    channels = packet.shape[1]
    layer = bias.shape[0] - 1
    started = [pltpu.make_async_copy(last_memory, memory_out.at[layer], cell_sems.at[0])]
    started[0].start()
    frame = xt.shape[1] // channels - 1
    run_layer(
        (either(first, part_of(xt, frame, channels), whole(packet)), whole(before)),
        (jnp.where(first, next_edge[...], packet[rows]), before[rows]),
        first_weights[...],
        bias[0],
        lambda at: before_memory[at, :],
        first_memory,
        first_hidden,
        first_gates,
        shifted,
        saves(last_gates, tiles, gates.at[1, layer], sems.at[0], started)
        + saves(last_hidden, hidden_tiles, hidden_out.at[layer], sems.at[2], started),
    )
    copy = pltpu.make_async_copy(first_memory, memory_out.at[0], cell_sems.at[1])
    copy.start()
    started.append(copy)
    for work in saves(first_gates, other_tiles, gates.at[1, 0], sems.at[1], started):
        work()
    for work in saves(first_hidden, other_hidden, hidden_out.at[0], sems.at[3], started):
        work()
    for copy in started:
        copy.wait()


def wavefront(frames, hidden_init, memory_init, weights, biases):
    steps, _, channels, rows, _ = frames.shape
    layers, gate_count, depth = weights.shape
    flat = channels * rows
    frames = in_hbm(frames.reshape(steps, flat, LANES))
    hidden_init = in_hbm(hidden_init.reshape(layers, flat, LANES))
    memory_init = in_hbm(memory_init.reshape(layers, flat, LANES))
    weights, biases = in_hbm(weights), in_hbm(biases)
    plane = (channels, LANES)
    sections = lax.axis_size("section")
    ahead = [(i, i + 1) for i in range(sections - 1)]

    def call(kernel, ins, outs, scratch=(), hbm=(), out_specs=None, aliases=None):
        return pl.pallas_call(
            kernel,
            in_specs=[HBM if i in hbm else VMEM for i in range(len(ins))],
            out_specs=out_specs or [VMEM] * len(outs),
            out_shape=outs,
            scratch_shapes=list(scratch),
            input_output_aliases=aliases or {},
            compiler_params=params(),
        )(*ins)

    state = pltpu.VMEM((rows,) + plane, bf16)
    state_and_edge = pltpu.VMEM((rows + 1,) + plane, bf16)
    memory = pltpu.VMEM((flat, LANES), f32)
    edge = pltpu.VMEM(plane, bf16)
    layer_weights = pltpu.VMEM((gate_count, depth), bf16)
    gate_rows = pltpu.VMEM((rows, gate_count, LANES), bf16)
    shifted = pltpu.VMEM((3, rows + 2, 2 * channels, LANES), bf16)
    gate_tiles = pltpu.VMEM((gate_count * rows, LANES), bf16)
    hidden_tiles = pltpu.VMEM((flat, LANES), bf16)
    pieces = gate_count * rows // 512

    xt, sent, first_edges, second_edges, cells, wide_bias, last_weights = call(
        prep_kernel,
        (frames, hidden_init, memory_init, biases, weights),
        [
            pltpu.VMEM((rows, (layers + steps) * channels, LANES), bf16),
            state,
            edge,
            edge,
            pltpu.VMEM((layers, flat, LANES), f32),
            pltpu.VMEM((layers, gate_count, LANES), f32),
            layer_weights,
        ],
        [
            pltpu.VMEM((layers + steps, flat, LANES), bf16),
            pltpu.VMEM((layers, gate_count), f32),
            pltpu.SemaphoreType.DMA((5,)),
        ],
        hbm=range(5),
    )
    packet = permuted(sent, "section", ahead)
    first_got = permuted(first_edges, "tile", swap_pairs(0))
    second_got = permuted(second_edges, "tile", swap_pairs(1))
    rough_gates, rough_memory, rough_hidden, first_weights = call(
        first_last_layer,
        (xt, last_weights, wide_bias, cells, weights),
        [gate_rows, memory, state, layer_weights],
        [shifted, pltpu.SemaphoreType.DMA],
        hbm=(4,),
    )
    packed, sent_edge, next_edge, taps, cell_edge = call(
        functools.partial(pack_kernel, rows),
        (first_edges, second_edges, first_got, second_got),
        [
            pltpu.VMEM((layers + 1,) + plane, bf16),
            edge,
            edge,
            pltpu.VMEM((3, 2 * channels, LANES), bf16),
            pltpu.VMEM((layers,) + plane, f32),
        ],
    )
    packet_edge = permuted(sent_edge, "section", ahead)
    last, last_memory, last_gates = call(
        mend_kernel,
        (taps, last_weights, wide_bias, cell_edge, rough_gates, rough_memory, rough_hidden),
        [state_and_edge, memory, gate_rows],
    )
    next_packet = permuted(last, "section", ahead)
    gates_shape = jax.ShapeDtypeStruct((steps, layers, gate_count * rows, LANES), bf16)
    before, before_memory, next_gates, next_memory, next_hidden, gates = call(
        middle_kernel,
        (
            xt, packet, packet_edge, packed, first_weights, last_weights, wide_bias, cells, cell_edge,
            last_gates, last, last_memory,
        ),
        [state_and_edge, memory, gate_rows, memory, state, gates_shape],
        [shifted, gate_rows, gate_tiles, gate_tiles, pltpu.SemaphoreType.DMA((2, pieces))],
        out_specs=[VMEM] * 5 + [HBM],
    )
    gates, hidden_out, memory_out = call(
        final_kernel,
        (
            xt, next_packet, next_edge, before, first_weights, wide_bias, before_memory,
            next_gates, next_memory, next_hidden, gates,
        ),
        [
            gates_shape,
            jax.ShapeDtypeStruct((layers, flat, LANES), bf16),
            jax.ShapeDtypeStruct((layers, flat, LANES), f32),
        ],
        [
            shifted, gate_rows, gate_tiles, gate_tiles, state, memory, hidden_tiles, hidden_tiles,
            pltpu.SemaphoreType.DMA((4, pieces)), pltpu.SemaphoreType.DMA((2,)),
        ],
        hbm=(10,),
        out_specs=[HBM] * 3,
        aliases={10: 0},
    )
    return (
        hidden_out.reshape(layers, 1, channels, rows, LANES),
        memory_out.reshape(layers, 1, channels, rows, LANES),
        gates.reshape(steps, layers, 1, gate_count, rows, LANES),
    )


def from_behind(block, axis, distance):
    devices = range(lax.axis_size(axis))
    route = [((i - distance) % len(devices), i) for i in devices]
    return lax.ppermute(block, axis, route)


def shifted(shard, axis, by):
    peers = lax.axis_size(axis)
    pairs = [(i, i + by) for i in range(peers) if 0 <= i + by < peers]
    return lax.ppermute(shard, axis, pairs)


def keep_if(condition, rim):
    return jnp.where(condition, rim, jnp.zeros_like(rim))


def with_rims(source_field):
    place = tile_place()
    row_place, column_place = (place // GRID_COLS, place % GRID_COLS)
    grid_rows = lax.axis_size("tile") // GRID_COLS
    upper_rim = from_behind(source_field[:, -1:, :], "tile", GRID_COLS)
    lower_rim = from_behind(source_field[:, :1, :], "tile", -GRID_COLS)
    upper_rim = keep_if(row_place > 0, upper_rim)
    lower_rim = keep_if(row_place < grid_rows - 1, lower_rim)
    heightened = jnp.concatenate([upper_rim, source_field, lower_rim], axis=1)
    left_rim = from_behind(heightened[:, :, -1:], "tile", 1)
    right_rim = from_behind(heightened[:, :, :1], "tile", -1)
    left_rim = keep_if(column_place > 0, left_rim)
    right_rim = keep_if(column_place < GRID_COLS - 1, right_rim)
    return jnp.concatenate([left_rim, heightened, right_rim], axis=2)


def hand_over(hidden_state):
    return shifted(hidden_state, "section", 1)


def advance(stacked, layer_weights, bias_row, memory):
    hidden_count = memory.shape[0]
    height = stacked.shape[1] - 2
    breadth = stacked.shape[2] - 2
    shifted_views = [
        stacked[:, row_offset : row_offset + height, column_offset : column_offset + breadth]
        for row_offset in range(3)
        for column_offset in range(3)
    ]
    patches = jnp.concatenate(shifted_views, axis=0).reshape(9 * stacked.shape[0], height * breadth)
    preact = jnp.dot(layer_weights, patches, preferred_element_type=jnp.float32) + bias_row[:, None]
    preact = preact.reshape(4, hidden_count, height, breadth)
    inflow = jax.nn.sigmoid(preact[0])
    forget = jax.nn.sigmoid(preact[1])
    outflow = jax.nn.sigmoid(preact[2])
    candidate = jnp.tanh(preact[3])
    memory = forget * memory + inflow * candidate
    hidden_state = (outflow * jnp.tanh(memory)).astype(jnp.bfloat16)
    opened = (
        jnp.stack([inflow, forget, outflow, candidate])
        .reshape(4 * hidden_count, height, breadth)
        .astype(jnp.bfloat16)
    )
    return (hidden_state, memory, opened)


def general_body(frames, hidden_init, memory_init, weights, biases):
    step_count = frames.shape[0]
    layer_count = weights.shape[0]
    channels = frames.shape[2]
    first_section = lax.axis_index("section") == 0
    saved_gates = []
    states = [hidden_init[layer_index, 0] for layer_index in range(layer_count)]
    memories = [memory_init[layer_index, 0] for layer_index in range(layer_count)]
    for moment in range(step_count):
        received = hand_over(states[-1])
        incoming = jnp.where(first_section, frames[moment, 0], received)
        padded = with_rims(jnp.concatenate([incoming] + states, axis=0))
        layer_stacks = [
            padded[layer_index * channels : (layer_index + 2) * channels]
            for layer_index in range(layer_count)
        ]
        fresh_states = []
        fresh_memories = []
        opened_step = []
        for layer_index in range(layer_count):
            hidden_state, memory, opened = advance(
                layer_stacks[layer_index],
                weights[layer_index],
                biases[layer_index],
                memories[layer_index],
            )
            fresh_states.append(hidden_state)
            fresh_memories.append(memory)
            opened_step.append(opened)
        states = fresh_states
        memories = fresh_memories
        saved_gates.append(jnp.stack(opened_step))
    hidden_out = jnp.stack(states)[:, None]
    memory_out = jnp.stack(memories)[:, None]
    gates_out = jnp.stack(saved_gates)[:, :, None]
    return (hidden_out, memory_out, gates_out)


def body(frames, hidden_init, memory_init, weights, biases):
    one_row = lax.axis_size("tile") == GRID_COLS
    if one_row and frames.shape[0] == 2 and weights.shape[0] == 2:
        return wavefront(frames, hidden_init, memory_init, weights, biases)
    return general_body(frames, hidden_init, memory_init, weights, biases)


def solution(mesh):
    in_specs = (
        P(None, ("member", "tile"), None, None, None),
        P("section", ("member", "tile"), None, None, None),
        P("section", ("member", "tile"), None, None, None),
        P("section", None, None),
        P("section", None),
    )
    out_specs = (
        P("section", ("member", "tile"), None, None, None),
        P("section", ("member", "tile"), None, None, None),
        P(None, "section", ("member", "tile"), None, None, None),
    )
    return jax.shard_map(body, mesh=mesh, in_specs=in_specs, out_specs=out_specs, check_vma=False)
```

```python
import functools

import jax
import jax.numpy as jnp
from jax import lax
from jax.experimental import pallas as pl
from jax.experimental.pallas import tpu as pltpu
from jax.sharding import PartitionSpec as P


GRID_COLS = 8
LANES = 128

bf16 = jnp.bfloat16
f32 = jnp.float32
VMEM = pl.BlockSpec(memory_space=pltpu.VMEM)
HBM = pl.BlockSpec(memory_space=pltpu.HBM)


def iota(shape, dim):
    return lax.broadcasted_iota(jnp.int32, shape, dim)


def params():
    return pltpu.CompilerParams(vmem_limit_bytes=24 * 2**20)


def in_vmem(array):
    return pltpu.with_memory_space_constraint(array, pltpu.VMEM)


def in_hbm(array):
    return pltpu.with_memory_space_constraint(array, pltpu.HBM)


def permuted(array, axis, pairs):
    return in_vmem(lax.ppermute(array, axis, pairs))


def tile_place():
    return (lax.axis_index("tile") + GRID_COLS + GRID_COLS // 2) % lax.axis_size("tile")


def swap_pairs(parity):
    count = lax.axis_size("tile")
    index = {(k + GRID_COLS + GRID_COLS // 2) % count: k for k in range(count)}
    pairs = []
    for place in range(parity, count, 2):
        one, other = index[place], index[(place + 1) % count]
        pairs += [(one, other), (other, one)]
    return pairs


def halves(value, base):
    return (value >> (base.bit_length() - 1), value & (base - 1))


def swap_matrix(rows, block, to_rows_first):
    size = rows * block
    m = iota((size, size), 0)
    n = iota((size, size), 1)
    if to_rows_first:
        m, n = n, m
    channel, row = halves(m, rows)
    other_row, other_channel = halves(n, block)
    return jnp.where((channel == other_channel) & (row == other_row), 1.0, 0.0).astype(bf16)


def turned(value, by):
    return pltpu.roll(value, by % LANES, 1)


def prep_kernel(
    frames, hidden, memory, bias, weights, xt, sent, first_edges, second_edges, cells, wide_bias, half_weights,
    raw, raw_bias, sems,
):
    layers, _, _ = hidden.shape
    rows, channels, _ = sent.shape
    copies = [
        pltpu.make_async_copy(hidden, raw.at[pl.ds(0, layers)], sems.at[0]),
        pltpu.make_async_copy(frames, raw.at[pl.ds(layers, frames.shape[0])], sems.at[1]),
        pltpu.make_async_copy(memory, cells, sems.at[2]),
        pltpu.make_async_copy(bias, raw_bias, sems.at[3]),
    ]
    half = channels // 2
    for q in range(4):
        source = weights.at[layers - 1, pl.ds(q * channels, half)]
        copies.append(pltpu.make_async_copy(source, half_weights.at[pl.ds(q * channels, half)], sems.at[4 + q]))
    copies[3].start()
    for copy in copies[:3] + copies[4:]:
        copy.start()
    copies[3].wait()
    blocks = [raw_bias[k : k + 1, q * channels : (q + 1) * channels] for k in range(layers) for q in range(4)]
    columns = jnp.concatenate(blocks + [jnp.zeros((channels - len(blocks), channels), f32)], axis=0).T
    for k in range(layers):
        for q in range(4):
            part = jnp.broadcast_to(columns[:, 4 * k + q : 4 * k + q + 1], (channels, LANES))
            wide_bias[k, q * channels : (q + 1) * channels] = part * (0.5 if q < 3 else 1.0)

    block = 256 // rows
    order = swap_matrix(rows, block, True)
    count = raw.shape[0]
    width = rows * LANES
    m = iota((width, LANES), 0)
    lane = iota((width, LANES), 1)
    near, row = halves(lane, rows)
    to_right = (lane < 2 * rows) & (m == row * LANES + (LANES - 2) + near)
    to_left = (lane < 2 * rows) & (m == row * LANES + 1 - near)
    select = jnp.concatenate(
        [jnp.where(to_right, 1.0, 0.0).astype(bf16), jnp.where(to_left, 1.0, 0.0).astype(bf16)], axis=1
    )
    for pair in range(0, count, 2):
        copies[pair // layers].wait()
        for group in range(channels // block):
            part = pl.ds(group * 256, 256)
            both = jnp.concatenate([raw[pair, part], raw[pair + 1, part]], axis=1)
            out = jnp.dot(order, both, preferred_element_type=f32).astype(bf16)
            for r in range(rows):
                for k in range(2):
                    piece = out[r * block : (r + 1) * block, k * LANES : (k + 1) * LANES]
                    at = (pair + k) * channels + group * block
                    xt[r, at : at + block] = piece
                    if pair + k == layers - 1:
                        sent[r, group * block : (group + 1) * block] = piece
    edge = 2 * rows
    m = iota((2 * LANES, 2 * LANES), 0)
    part, place = halves(m, LANES)
    layer_of, place = halves(place, edge)
    row, side = halves(place, 2)
    target = side * LANES + (count + layer_of) * edge + part * rows + row
    spread = (layer_of < layers) & (iota((2 * LANES, 2 * LANES), 1) == target)
    spread = jnp.where(spread, 1.0, 0.0).astype(bf16)
    copies[2].wait()
    lane_pair = iota((channels, LANES), 1) >> 1
    cell_columns = jnp.zeros((channels, LANES), f32)
    for layer in range(layers):
        for r in range(rows):
            moved = turned(cells[layer, pl.ds(r, channels, stride=rows), :], layer * edge + 2 * r + 1)
            cell_columns = jnp.where(lane_pair == layer * rows + r, moved, cell_columns)
    high = cell_columns.astype(bf16)
    low = (cell_columns - high.astype(f32)).astype(bf16)
    wide = jnp.concatenate([xt[r] for r in range(rows)], axis=1)
    edges = jnp.dot(wide, select, preferred_element_type=f32)
    out = jnp.dot(jnp.concatenate([high, low], axis=1), spread, preferred_element_type=f32)
    right, left = out[:, :LANES], out[:, LANES:]
    for k in range(count):
        part = edges[k * channels : (k + 1) * channels]
        right += turned(part[:, :LANES], k * edge)
        left += turned(part[:, LANES:], k * edge)
    even = tile_place() % 2 == 0
    first_edges[...] = jnp.where(even, right, left).astype(bf16)
    second_edges[...] = jnp.where(even, left, right).astype(bf16)
    for copy in copies[4:]:
        copy.wait()


def cell_step(pre, bias, memory):
    channels = memory.shape[0]

    def gate(q):
        part = slice(q * channels, (q + 1) * channels)
        if q == 3:
            return jnp.tanh(pre[part] + bias[part])
        return jnp.tanh(pre[part] * 0.5 + bias[part]) * 0.5 + 0.5

    inflow, forget, outflow, candidate = gate(0), gate(1), gate(2), gate(3)
    memory = forget * memory + inflow * candidate
    hidden = (outflow * jnp.tanh(memory)).astype(bf16)
    return (inflow, forget, outflow, candidate), memory, hidden


def run_layer(sources, edge_columns, weights, bias, memory_of, memory_out, hidden_rows, gate_rows, shifted, beside=()):
    rows = shifted.shape[1] - 2
    channels = shifted.shape[2] // 2
    lane = iota((channels, LANES), 1)
    blank = jnp.zeros((2 * channels, LANES), bf16)
    for b in range(3):
        shifted[b, 0] = blank
        shifted[b, rows + 1] = blank

    def build(r):
        for k in range(2):
            part = slice(k * channels, (k + 1) * channels)
            x = sources[k](r)
            if edge_columns is None:
                before = after = jnp.zeros_like(x)
            else:
                before = turned(edge_columns[k], -2 * rows - r)
                after = turned(edge_columns[k], -1 - 3 * rows - r)
            shifted[1, r + 1, part] = x
            shifted[0, r + 1, part] = jnp.where(lane == 0, before, turned(x, 1))
            shifted[2, r + 1, part] = jnp.where(lane == LANES - 1, after, turned(x, -1))

    for r in range(rows):
        build(r)
    beside = list(beside)
    tiles = rows // 2
    share = -(-len(beside) // tiles)
    parts = 1 if beside else 2
    size = channels // parts
    for low in range(0, channels, size):
        chosen = [slice(q * channels + low, q * channels + low + size) for q in range(4)]
        if parts == 1:
            part_weights, part_bias = weights, bias
        else:
            part_weights = weights(low)
            part_bias = jnp.concatenate([bias[c] for c in chosen], axis=0)
        for j in range(tiles):
            for work in beside[j * share : (j + 1) * share]:
                work()
            patches = jnp.concatenate(
                [
                    jnp.concatenate([shifted[b, 2 * j + a], shifted[b, 2 * j + a + 1]], axis=1)
                    for a in range(3)
                    for b in range(3)
                ],
                axis=0,
            )
            total = jnp.dot(part_weights, patches, preferred_element_type=f32)
            for k in range(2):
                r = 2 * j + k
                at = pl.ds(r + rows * low, size, stride=rows)
                gates, memory, hidden = cell_step(total[:, k * LANES : (k + 1) * LANES], part_bias, memory_of(at))
                memory_out[at, :] = memory
                hidden_rows[r, low : low + size] = hidden
                for q in range(4):
                    gate_rows[r, chosen[q]] = gates[q].astype(bf16)


def edge_step(columns, weights, bias, memory, rows):
    channels = memory.shape[0]
    lane = iota((2 * channels, LANES), 1)
    parts = []
    pixel_row = lane & (rows - 1)
    for a in range(3):
        row = pixel_row + (a - 1)
        for b in range(3):
            moved = turned(columns[b], 1 - a)
            parts.append(jnp.where((row >= 0) & (row < rows), moved, jnp.zeros_like(moved)))
    total = jnp.dot(weights, jnp.concatenate(parts, axis=0), preferred_element_type=f32)
    return cell_step(total, bias, memory)


def outer_columns(hidden, rows):
    lane = iota(hidden.shape, 1)
    place = tile_place() % GRID_COLS
    inside = ((lane < rows) & (place > 0)) | ((lane >= rows) & (lane < 2 * rows) & (place < GRID_COLS - 1))
    return turned(jnp.where(inside, hidden, jnp.zeros_like(hidden)), 2 * rows)


def restore(order, source, target, first):
    rows = source.shape[0]
    block = 256 // rows
    both = []
    for at in (first // rows, first // rows + block):
        both.append(jnp.concatenate([source[r, at : at + block] for r in range(rows)], axis=0))
    out = jnp.dot(order, jnp.concatenate(both, axis=1), preferred_element_type=f32).astype(bf16)
    target[first : first + 256] = out[:, :LANES]
    target[first + 256 : first + 512] = out[:, LANES:]


def saves(order, source, tiles, out, sems, started):
    def piece(first):
        def work():
            restore(order, source, tiles, first)
            part = pl.ds(first, 512)
            copy = pltpu.make_async_copy(tiles.at[part], out.at[part], sems.at[first // 512])
            copy.start()
            started.append(copy)

        return work

    return [piece(first) for first in range(0, tiles.shape[0], 512)]


def part_of(ref, k, channels):
    def load(r):
        return ref[r, k * channels : (k + 1) * channels]

    return load


def either(condition, one, other):
    def load(r):
        return jnp.where(condition, one(r), other(r))

    return load


def whole(ref):
    return lambda r: ref[r]


def first_last_layer(
    xt, bias, cells, weights, _, gate_rows, memory, hidden, first_weights, last_weights, shifted, sems
):
    layer = bias.shape[0] - 1
    channels = hidden.shape[1]
    half = channels // 2
    copies = []
    for q in range(4):
        part = pl.ds(q * channels + half, half)
        copies.append(pltpu.make_async_copy(weights.at[layer, part], last_weights.at[part], sems.at[q]))
    copies.append(pltpu.make_async_copy(weights.at[0], first_weights, sems.at[4]))
    for copy in copies:
        copy.start()

    def weights_of(low):
        if low > 0:
            for copy in copies[:4]:
                copy.wait()
        parts = [last_weights[q * channels + low : q * channels + low + half] for q in range(4)]
        return jnp.concatenate(parts, axis=0)

    run_layer(
        (part_of(xt, layer - 1, channels), part_of(xt, layer, channels)),
        None,
        weights_of,
        bias[layer],
        lambda at: cells[layer, at, :],
        memory,
        hidden,
        gate_rows,
        shifted,
    )
    copies[4].wait()


def pack_kernel(rows, first_own, second_own, first_got, second_got, packed, sent, next_edge, taps, cell_edge):
    channels = sent.shape[0]
    layers = cell_edge.shape[0]
    layer = layers - 1
    edge = 2 * rows
    even = tile_place() % 2 == 0
    own_right = jnp.where(even, first_own[...], second_own[...])
    own_left = jnp.where(even, second_own[...], first_own[...])
    from_left = jnp.where(even, second_got[...], first_got[...])
    from_right = jnp.where(even, first_got[...], second_got[...])
    from_left = jnp.where(tile_place() > 0, from_left, jnp.zeros_like(from_left))
    from_right = jnp.where(tile_place() < GRID_COLS - 1, from_right, jnp.zeros_like(from_right))
    lane = iota((channels, LANES), 1)

    def laid(k, pieces):
        out = jnp.zeros((channels, LANES), bf16)
        for slot, (value, block) in enumerate(pieces):
            value = turned(value, (slot - block) * rows - k * edge)
            out = jnp.where((lane >= slot * rows) & (lane < (slot + 1) * rows), value, out)
        return out

    outer = [(from_left, 0), (own_right, 1), (from_left, 1), (from_right, 1), (own_left, 1), (from_right, 0)]
    for k in range(layers + 1):
        packed[k] = laid(k, outer)
    sent[...] = packed[layer]
    next_edge[...] = laid(layers + 1, outer)
    inner = [
        [(from_left, 0), (own_right, 1), (from_left, 1), (own_right, 0)],
        [(from_left, 1), (from_right, 1), (own_left, 1), (own_right, 1)],
        [(own_left, 1), (from_right, 0), (own_left, 0), (from_right, 1)],
    ]
    for b in range(3):
        for k in range(2):
            taps[b, k * channels : (k + 1) * channels] = laid(layer - 1 + k, inner[b])
    for k in range(layers):
        high, low = (
            laid(layers + 2 + k, [(value, part) for value in (from_left, from_right, own_left, own_right)])
            for part in range(2)
        )
        cell_edge[k] = high.astype(f32) + low.astype(f32)


def mend_kernel(taps, last_weights, bias, cell_edge, gate_rows, memory, hidden, last, new_memory, new_gates):
    rows, channels, _ = hidden.shape
    layer = bias.shape[0] - 1
    gates, edge_memory, edge_hidden = edge_step(
        [taps[b] for b in range(3)], last_weights[...], bias[layer], cell_edge[layer], rows
    )
    last[rows] = outer_columns(edge_hidden, rows)
    gates = jnp.concatenate([gate.astype(bf16) for gate in gates], axis=0)

    def mended(value, column, r):
        lane = iota(value.shape, 1)
        value = jnp.where(lane == 0, turned(column, -2 * rows - r), value)
        return jnp.where(lane == LANES - 1, turned(column, -1 - 3 * rows - r), value)

    for r in range(rows):
        last[r] = mended(hidden[r], edge_hidden, r)
    for r in range(rows):
        at = pl.ds(r, channels, stride=rows)
        new_memory[at, :] = mended(memory[at, :], edge_memory, r)
        new_gates[r] = mended(gate_rows[r], gates, r)


def middle_kernel(
    xt, packet, packet_edge, packed, first_weights, last_weights, bias, cells, cell_edge, gate_rows, last, last_memory,
    before, before_memory, next_gates, next_memory, next_hidden, gates,
    shifted, first_gates, tiles, other_tiles, sems,
):
    first = lax.axis_index("section") == 0
    rows, channels, _ = packet.shape
    layers = bias.shape[0]
    order = swap_matrix(rows, 256 // rows, False)
    started = []
    edges = (jnp.where(first, packed[layers], packet_edge[...]), packed[0])
    run_layer(
        (either(first, part_of(xt, layers, channels), whole(packet)), part_of(xt, 0, channels)),
        edges,
        first_weights[...],
        bias[0],
        lambda at: cells[0, at, :],
        before_memory,
        before,
        first_gates,
        shifted,
        saves(order, gate_rows, tiles, gates.at[0, layers - 1], sems.at[0], started),
    )
    wide = jnp.concatenate(edges, axis=0)
    columns = [turned(wide, -2 * rows * b) for b in range(3)]
    _, _, hidden = edge_step(columns, first_weights[...], bias[0], cell_edge[0], rows)
    before[rows] = outer_columns(hidden, rows)
    run_layer(
        (whole(before), whole(last)),
        (before[rows], last[rows]),
        last_weights[...],
        bias[layers - 1],
        lambda at: last_memory[at, :],
        next_memory,
        next_hidden,
        next_gates,
        shifted,
        saves(order, first_gates, other_tiles, gates.at[0, 0], sems.at[1], started),
    )
    for copy in started:
        copy.wait()


def final_kernel(
    xt, packet, next_edge, before, first_weights, bias, before_memory, last_gates, last_memory, last_hidden, _,
    gates, hidden_out, memory_out,
    shifted, first_gates, tiles, other_tiles, first_hidden, first_memory, hidden_tiles, other_hidden, sems, cell_sems,
):
    first = lax.axis_index("section") == 0
    rows = packet.shape[0] - 1
    channels = packet.shape[1]
    layer = bias.shape[0] - 1
    order = swap_matrix(rows, 256 // rows, False)
    started = [pltpu.make_async_copy(last_memory, memory_out.at[layer], cell_sems.at[0])]
    started[0].start()
    frame = xt.shape[1] // channels - 1
    run_layer(
        (either(first, part_of(xt, frame, channels), whole(packet)), whole(before)),
        (jnp.where(first, next_edge[...], packet[rows]), before[rows]),
        first_weights[...],
        bias[0],
        lambda at: before_memory[at, :],
        first_memory,
        first_hidden,
        first_gates,
        shifted,
        saves(order, last_gates, tiles, gates.at[1, layer], sems.at[0], started)
        + saves(order, last_hidden, hidden_tiles, hidden_out.at[layer], sems.at[2], started),
    )
    copy = pltpu.make_async_copy(first_memory, memory_out.at[0], cell_sems.at[1])
    copy.start()
    started.append(copy)
    for work in saves(order, first_gates, other_tiles, gates.at[1, 0], sems.at[1], started):
        work()
    for work in saves(order, first_hidden, other_hidden, hidden_out.at[0], sems.at[3], started):
        work()
    for copy in started:
        copy.wait()


def wavefront(frames, hidden_init, memory_init, weights, biases):
    steps, _, channels, rows, _ = frames.shape
    layers, gate_count, depth = weights.shape
    flat = channels * rows
    frames = in_hbm(frames.reshape(steps, flat, LANES))
    hidden_init = in_hbm(hidden_init.reshape(layers, flat, LANES))
    memory_init = in_hbm(memory_init.reshape(layers, flat, LANES))
    weights, biases = in_hbm(weights), in_hbm(biases)
    plane = (channels, LANES)
    sections = lax.axis_size("section")
    ahead = [(i, (i + 1) % sections) for i in range(sections)]

    def call(kernel, ins, outs, scratch=(), hbm=(), out_specs=None, aliases=None):
        return pl.pallas_call(
            kernel,
            in_specs=[HBM if i in hbm else VMEM for i in range(len(ins))],
            out_specs=out_specs or [VMEM] * len(outs),
            out_shape=outs,
            scratch_shapes=list(scratch),
            input_output_aliases=aliases or {},
            compiler_params=params(),
        )(*ins)

    state = pltpu.VMEM((rows,) + plane, bf16)
    state_and_edge = pltpu.VMEM((rows + 1,) + plane, bf16)
    memory = pltpu.VMEM((flat, LANES), f32)
    edge = pltpu.VMEM(plane, bf16)
    layer_weights = pltpu.VMEM((gate_count, depth), bf16)
    gate_rows = pltpu.VMEM((rows, gate_count, LANES), bf16)
    shifted = pltpu.VMEM((3, rows + 2, 2 * channels, LANES), bf16)
    gate_tiles = pltpu.VMEM((gate_count * rows, LANES), bf16)
    hidden_tiles = pltpu.VMEM((flat, LANES), bf16)
    pieces = gate_count * rows // 512

    xt, sent, first_edges, second_edges, cells, wide_bias, half_weights = call(
        prep_kernel,
        (frames, hidden_init, memory_init, biases, weights),
        [
            pltpu.VMEM((rows, (layers + steps) * channels, LANES), bf16),
            state,
            edge,
            edge,
            pltpu.VMEM((layers, flat, LANES), f32),
            pltpu.VMEM((layers, gate_count, LANES), f32),
            layer_weights,
        ],
        [
            pltpu.VMEM((layers + steps, flat, LANES), bf16),
            pltpu.VMEM((layers, gate_count), f32),
            pltpu.SemaphoreType.DMA((8,)),
        ],
        hbm=range(5),
    )
    packet = permuted(sent, "section", ahead)
    first_got = permuted(first_edges, "tile", swap_pairs(0))
    second_got = permuted(second_edges, "tile", swap_pairs(1))
    rough_gates, rough_memory, rough_hidden, first_weights, last_weights = call(
        first_last_layer,
        (xt, wide_bias, cells, weights, half_weights),
        [gate_rows, memory, state, layer_weights, layer_weights],
        [shifted, pltpu.SemaphoreType.DMA((5,))],
        hbm=(3,),
        aliases={4: 4},
    )
    packed, sent_edge, next_edge, taps, cell_edge = call(
        functools.partial(pack_kernel, rows),
        (first_edges, second_edges, first_got, second_got),
        [
            pltpu.VMEM((layers + 1,) + plane, bf16),
            edge,
            edge,
            pltpu.VMEM((3, 2 * channels, LANES), bf16),
            pltpu.VMEM((layers,) + plane, f32),
        ],
    )
    packet_edge = permuted(sent_edge, "section", ahead)
    last, last_memory, last_gates = call(
        mend_kernel,
        (taps, last_weights, wide_bias, cell_edge, rough_gates, rough_memory, rough_hidden),
        [state_and_edge, memory, gate_rows],
    )
    next_packet = permuted(last, "section", ahead)
    gates_shape = jax.ShapeDtypeStruct((steps, layers, gate_count * rows, LANES), bf16)
    before, before_memory, next_gates, next_memory, next_hidden, gates = call(
        middle_kernel,
        (
            xt, packet, packet_edge, packed, first_weights, last_weights, wide_bias, cells, cell_edge,
            last_gates, last, last_memory,
        ),
        [state_and_edge, memory, gate_rows, memory, state, gates_shape],
        [shifted, gate_rows, gate_tiles, gate_tiles, pltpu.SemaphoreType.DMA((2, pieces))],
        out_specs=[VMEM] * 5 + [HBM],
    )
    gates, hidden_out, memory_out = call(
        final_kernel,
        (
            xt, next_packet, next_edge, before, first_weights, wide_bias, before_memory,
            next_gates, next_memory, next_hidden, gates,
        ),
        [
            gates_shape,
            jax.ShapeDtypeStruct((layers, flat, LANES), bf16),
            jax.ShapeDtypeStruct((layers, flat, LANES), f32),
        ],
        [
            shifted, gate_rows, gate_tiles, gate_tiles, state, memory, hidden_tiles, hidden_tiles,
            pltpu.SemaphoreType.DMA((4, pieces)), pltpu.SemaphoreType.DMA((2,)),
        ],
        hbm=(10,),
        out_specs=[HBM] * 3,
        aliases={10: 0},
    )
    return (
        hidden_out.reshape(layers, 1, channels, rows, LANES),
        memory_out.reshape(layers, 1, channels, rows, LANES),
        gates.reshape(steps, layers, 1, gate_count, rows, LANES),
    )


def from_behind(block, axis, distance):
    devices = range(lax.axis_size(axis))
    route = [((i - distance) % len(devices), i) for i in devices]
    return lax.ppermute(block, axis, route)


def shifted(shard, axis, by):
    peers = lax.axis_size(axis)
    pairs = [(i, i + by) for i in range(peers) if 0 <= i + by < peers]
    return lax.ppermute(shard, axis, pairs)


def keep_if(condition, rim):
    return jnp.where(condition, rim, jnp.zeros_like(rim))


def with_rims(source_field):
    place = tile_place()
    row_place, column_place = (place // GRID_COLS, place % GRID_COLS)
    grid_rows = lax.axis_size("tile") // GRID_COLS
    upper_rim = from_behind(source_field[:, -1:, :], "tile", GRID_COLS)
    lower_rim = from_behind(source_field[:, :1, :], "tile", -GRID_COLS)
    upper_rim = keep_if(row_place > 0, upper_rim)
    lower_rim = keep_if(row_place < grid_rows - 1, lower_rim)
    heightened = jnp.concatenate([upper_rim, source_field, lower_rim], axis=1)
    left_rim = from_behind(heightened[:, :, -1:], "tile", 1)
    right_rim = from_behind(heightened[:, :, :1], "tile", -1)
    left_rim = keep_if(column_place > 0, left_rim)
    right_rim = keep_if(column_place < GRID_COLS - 1, right_rim)
    return jnp.concatenate([left_rim, heightened, right_rim], axis=2)


def hand_over(hidden_state):
    return shifted(hidden_state, "section", 1)


def advance(stacked, layer_weights, bias_row, memory):
    hidden_count = memory.shape[0]
    height = stacked.shape[1] - 2
    breadth = stacked.shape[2] - 2
    shifted_views = [
        stacked[:, row_offset : row_offset + height, column_offset : column_offset + breadth]
        for row_offset in range(3)
        for column_offset in range(3)
    ]
    patches = jnp.concatenate(shifted_views, axis=0).reshape(9 * stacked.shape[0], height * breadth)
    preact = jnp.dot(layer_weights, patches, preferred_element_type=jnp.float32) + bias_row[:, None]
    preact = preact.reshape(4, hidden_count, height, breadth)
    inflow = jax.nn.sigmoid(preact[0])
    forget = jax.nn.sigmoid(preact[1])
    outflow = jax.nn.sigmoid(preact[2])
    candidate = jnp.tanh(preact[3])
    memory = forget * memory + inflow * candidate
    hidden_state = (outflow * jnp.tanh(memory)).astype(jnp.bfloat16)
    opened = (
        jnp.stack([inflow, forget, outflow, candidate])
        .reshape(4 * hidden_count, height, breadth)
        .astype(jnp.bfloat16)
    )
    return (hidden_state, memory, opened)


def general_body(frames, hidden_init, memory_init, weights, biases):
    step_count = frames.shape[0]
    layer_count = weights.shape[0]
    channels = frames.shape[2]
    first_section = lax.axis_index("section") == 0
    saved_gates = []
    states = [hidden_init[layer_index, 0] for layer_index in range(layer_count)]
    memories = [memory_init[layer_index, 0] for layer_index in range(layer_count)]
    for moment in range(step_count):
        received = hand_over(states[-1])
        incoming = jnp.where(first_section, frames[moment, 0], received)
        padded = with_rims(jnp.concatenate([incoming] + states, axis=0))
        layer_stacks = [
            padded[layer_index * channels : (layer_index + 2) * channels]
            for layer_index in range(layer_count)
        ]
        fresh_states = []
        fresh_memories = []
        opened_step = []
        for layer_index in range(layer_count):
            hidden_state, memory, opened = advance(
                layer_stacks[layer_index],
                weights[layer_index],
                biases[layer_index],
                memories[layer_index],
            )
            fresh_states.append(hidden_state)
            fresh_memories.append(memory)
            opened_step.append(opened)
        states = fresh_states
        memories = fresh_memories
        saved_gates.append(jnp.stack(opened_step))
    hidden_out = jnp.stack(states)[:, None]
    memory_out = jnp.stack(memories)[:, None]
    gates_out = jnp.stack(saved_gates)[:, :, None]
    return (hidden_out, memory_out, gates_out)


def body(frames, hidden_init, memory_init, weights, biases):
    one_row = lax.axis_size("tile") == GRID_COLS
    if one_row and frames.shape[0] == 2 and weights.shape[0] == 2:
        return wavefront(frames, hidden_init, memory_init, weights, biases)
    return general_body(frames, hidden_init, memory_init, weights, biases)


def solution(mesh):
    in_specs = (
        P(None, ("member", "tile"), None, None, None),
        P("section", ("member", "tile"), None, None, None),
        P("section", ("member", "tile"), None, None, None),
        P("section", None, None),
        P("section", None),
    )
    out_specs = (
        P("section", ("member", "tile"), None, None, None),
        P("section", ("member", "tile"), None, None, None),
        P(None, "section", ("member", "tile"), None, None, None),
    )
    return jax.shard_map(body, mesh=mesh, in_specs=in_specs, out_specs=out_specs, check_vma=False)
```

```python
import functools

import jax
import jax.numpy as jnp
from jax import lax
from jax.experimental import pallas as pl
from jax.experimental.pallas import tpu as pltpu
from jax.sharding import PartitionSpec as P


GRID_COLS = 8
LANES = 128

bf16 = jnp.bfloat16
f32 = jnp.float32
VMEM = pl.BlockSpec(memory_space=pltpu.VMEM)
HBM = pl.BlockSpec(memory_space=pltpu.HBM)


def iota(shape, dim):
    return lax.broadcasted_iota(jnp.int32, shape, dim)


def params():
    return pltpu.CompilerParams(vmem_limit_bytes=24 * 2**20)


def in_vmem(array):
    return pltpu.with_memory_space_constraint(array, pltpu.VMEM)


def in_hbm(array):
    return pltpu.with_memory_space_constraint(array, pltpu.HBM)


def permuted(array, axis, pairs):
    return in_vmem(lax.ppermute(array, axis, pairs))


def tile_place():
    return (lax.axis_index("tile") + GRID_COLS + GRID_COLS // 2) % lax.axis_size("tile")


def swap_pairs(parity):
    count = lax.axis_size("tile")
    index = {(k + GRID_COLS + GRID_COLS // 2) % count: k for k in range(count)}
    pairs = []
    for place in range(parity, count, 2):
        one, other = index[place], index[(place + 1) % count]
        pairs += [(one, other), (other, one)]
    return pairs


def halves(value, base):
    return (value >> (base.bit_length() - 1), value & (base - 1))


def swap_matrix(rows, block, to_rows_first):
    size = rows * block
    m = iota((size, size), 0)
    n = iota((size, size), 1)
    if to_rows_first:
        m, n = n, m
    channel, row = halves(m, rows)
    other_row, other_channel = halves(n, block)
    return jnp.where((channel == other_channel) & (row == other_row), 1.0, 0.0).astype(bf16)


def turned(value, by):
    return pltpu.roll(value, by % LANES, 1)


def prep_kernel(
    frames, hidden, memory, bias, weights, xt, sent, first_edges, second_edges, cells, wide_bias, last_weights,
    raw, raw_bias, sems,
):
    layers, _, _ = hidden.shape
    rows, channels, _ = sent.shape
    copies = [
        pltpu.make_async_copy(hidden, raw.at[pl.ds(0, layers)], sems.at[0]),
        pltpu.make_async_copy(frames, raw.at[pl.ds(layers, frames.shape[0])], sems.at[1]),
        pltpu.make_async_copy(memory, cells, sems.at[2]),
        pltpu.make_async_copy(bias, raw_bias, sems.at[3]),
    ]
    copies.append(pltpu.make_async_copy(weights.at[layers - 1], last_weights, sems.at[4]))
    copies[3].start()
    for copy in copies[:3] + copies[4:]:
        copy.start()
    copies[3].wait()
    blocks = [raw_bias[k : k + 1, q * channels : (q + 1) * channels] for k in range(layers) for q in range(4)]
    columns = jnp.concatenate(blocks + [jnp.zeros((channels - len(blocks), channels), f32)], axis=0).T
    for k in range(layers):
        for q in range(4):
            part = jnp.broadcast_to(columns[:, 4 * k + q : 4 * k + q + 1], (channels, LANES))
            wide_bias[k, q * channels : (q + 1) * channels] = part * (0.5 if q < 3 else 1.0)

    block = 256 // rows
    order = swap_matrix(rows, block, True)
    count = raw.shape[0]
    width = rows * LANES
    m = iota((width, LANES), 0)
    lane = iota((width, LANES), 1)
    near, row = halves(lane, rows)
    to_right = (lane < 2 * rows) & (m == row * LANES + (LANES - 2) + near)
    to_left = (lane < 2 * rows) & (m == row * LANES + 1 - near)
    select = jnp.concatenate(
        [jnp.where(to_right, 1.0, 0.0).astype(bf16), jnp.where(to_left, 1.0, 0.0).astype(bf16)], axis=1
    )
    for pair in range(0, count, 2):
        copies[pair // layers].wait()
        for group in range(channels // block):
            part = pl.ds(group * 256, 256)
            both = jnp.concatenate([raw[pair, part], raw[pair + 1, part]], axis=1)
            out = jnp.dot(order, both, preferred_element_type=f32).astype(bf16)
            for r in range(rows):
                for k in range(2):
                    piece = out[r * block : (r + 1) * block, k * LANES : (k + 1) * LANES]
                    at = (pair + k) * channels + group * block
                    xt[r, at : at + block] = piece
                    if pair + k == layers - 1:
                        sent[r, group * block : (group + 1) * block] = piece
    edge = 2 * rows
    m = iota((2 * LANES, 2 * LANES), 0)
    part, place = halves(m, LANES)
    layer_of, place = halves(place, edge)
    row, side = halves(place, 2)
    target = side * LANES + (count + layer_of) * edge + part * rows + row
    spread = (layer_of < layers) & (iota((2 * LANES, 2 * LANES), 1) == target)
    spread = jnp.where(spread, 1.0, 0.0).astype(bf16)
    copies[2].wait()
    lane_pair = iota((channels, LANES), 1) >> 1
    cell_columns = jnp.zeros((channels, LANES), f32)
    for layer in range(layers):
        for r in range(rows):
            moved = turned(cells[layer, pl.ds(r, channels, stride=rows), :], layer * edge + 2 * r + 1)
            cell_columns = jnp.where(lane_pair == layer * rows + r, moved, cell_columns)
    high = cell_columns.astype(bf16)
    low = (cell_columns - high.astype(f32)).astype(bf16)
    wide = jnp.concatenate([xt[r] for r in range(rows)], axis=1)
    edges = jnp.dot(wide, select, preferred_element_type=f32)
    out = jnp.dot(jnp.concatenate([high, low], axis=1), spread, preferred_element_type=f32)
    right, left = out[:, :LANES], out[:, LANES:]
    for k in range(count):
        part = edges[k * channels : (k + 1) * channels]
        right += turned(part[:, :LANES], k * edge)
        left += turned(part[:, LANES:], k * edge)
    even = tile_place() % 2 == 0
    first_edges[...] = jnp.where(even, right, left).astype(bf16)
    second_edges[...] = jnp.where(even, left, right).astype(bf16)
    copies[4].wait()


def cell_step(pre, bias, memory):
    channels = memory.shape[0]

    def gate(q):
        part = slice(q * channels, (q + 1) * channels)
        if q == 3:
            return jnp.tanh(pre[part] + bias[part])
        return jnp.tanh(pre[part] * 0.5 + bias[part]) * 0.5 + 0.5

    inflow, forget, outflow, candidate = gate(0), gate(1), gate(2), gate(3)
    memory = forget * memory + inflow * candidate
    hidden = (outflow * jnp.tanh(memory)).astype(bf16)
    return (inflow, forget, outflow, candidate), memory, hidden


def run_layer(sources, edge_columns, weights, bias, memory_of, memory_out, hidden_rows, gate_rows, shifted, beside=()):
    rows = shifted.shape[1] - 2
    channels = shifted.shape[2] // 2
    lane = iota((channels, LANES), 1)
    blank = jnp.zeros((2 * channels, LANES), bf16)
    for b in range(3):
        shifted[b, 0] = blank
        shifted[b, rows + 1] = blank

    def build(r):
        for k in range(2):
            part = slice(k * channels, (k + 1) * channels)
            x = sources[k](r)
            if edge_columns is None:
                before = after = jnp.zeros_like(x)
            else:
                before = turned(edge_columns[k], -2 * rows - r)
                after = turned(edge_columns[k], -1 - 3 * rows - r)
            shifted[1, r + 1, part] = x
            shifted[0, r + 1, part] = jnp.where(lane == 0, before, turned(x, 1))
            shifted[2, r + 1, part] = jnp.where(lane == LANES - 1, after, turned(x, -1))

    for r in range(rows):
        build(r)
    tiles = rows // 2
    parts = 1 if beside else 2
    size = channels // parts
    for low in range(0, channels, size):
        chosen = [slice(q * channels + low, q * channels + low + size) for q in range(4)]
        if parts == 1:
            part_weights, part_bias = weights, bias
        else:
            part_weights = weights(low)
            part_bias = jnp.concatenate([bias[c] for c in chosen], axis=0)
        for j in range(tiles):
            for work in beside[j] if beside else ():
                work()
            patches = jnp.concatenate(
                [
                    jnp.concatenate([shifted[b, 2 * j + a], shifted[b, 2 * j + a + 1]], axis=1)
                    for a in range(3)
                    for b in range(3)
                ],
                axis=0,
            )
            total = jnp.dot(part_weights, patches, preferred_element_type=f32)
            for k in range(2):
                r = 2 * j + k
                at = pl.ds(r + rows * low, size, stride=rows)
                gates, memory, hidden = cell_step(total[:, k * LANES : (k + 1) * LANES], part_bias, memory_of(at))
                memory_out[at, :] = memory
                hidden_rows[r, low : low + size] = hidden
                for q in range(4):
                    gate_rows[r, chosen[q]] = gates[q].astype(bf16)


def edge_step(columns, weights, bias, memory, rows):
    channels = memory.shape[0]
    lane = iota((2 * channels, LANES), 1)
    parts = []
    pixel_row = lane & (rows - 1)
    for a in range(3):
        row = pixel_row + (a - 1)
        for b in range(3):
            moved = turned(columns[b], 1 - a)
            parts.append(jnp.where((row >= 0) & (row < rows), moved, jnp.zeros_like(moved)))
    total = jnp.dot(weights, jnp.concatenate(parts, axis=0), preferred_element_type=f32)
    return cell_step(total, bias, memory)


def outer_columns(hidden, rows):
    lane = iota(hidden.shape, 1)
    place = tile_place() % GRID_COLS
    inside = ((lane < rows) & (place > 0)) | ((lane >= rows) & (lane < 2 * rows) & (place < GRID_COLS - 1))
    return turned(jnp.where(inside, hidden, jnp.zeros_like(hidden)), 2 * rows)


def restore(order, source, target, first):
    rows = source.shape[0]
    block = 256 // rows
    both = []
    for at in (first // rows, first // rows + block):
        both.append(jnp.concatenate([source[r, at : at + block] for r in range(rows)], axis=0))
    out = jnp.dot(order, jnp.concatenate(both, axis=1), preferred_element_type=f32).astype(bf16)
    target[first : first + 256] = out[:, :LANES]
    target[first + 256 : first + 512] = out[:, LANES:]


def saves(order, source, tiles, out, sems, started):
    def piece(first):
        def work():
            restore(order, source, tiles, first)
            part = pl.ds(first, 512)
            copy = pltpu.make_async_copy(tiles.at[part], out.at[part], sems.at[first // 512])
            copy.start()
            started.append(copy)

        return work

    return [piece(first) for first in range(0, tiles.shape[0], 512)]


def dealt(works, hands):
    share = -(-len(works) // hands)
    return [works[j * share : (j + 1) * share] for j in range(hands)]


def mended(value, column, r, rows):
    lane = iota(value.shape, 1)
    value = jnp.where(lane == 0, turned(column, -2 * rows - r), value)
    return jnp.where(lane == LANES - 1, turned(column, -1 - 3 * rows - r), value)


def part_of(ref, k, channels):
    def load(r):
        return ref[r, k * channels : (k + 1) * channels]

    return load


def either(condition, one, other):
    def load(r):
        return jnp.where(condition, one(r), other(r))

    return load


def whole(ref):
    return lambda r: ref[r]


def first_last_layer(xt, bias, cells, weights, last_weights, gate_rows, memory, hidden, first_weights, shifted, sem):
    layer = bias.shape[0] - 1
    channels = hidden.shape[1]
    copy = pltpu.make_async_copy(weights.at[0], first_weights, sem)
    copy.start()
    run_layer(
        (part_of(xt, layer - 1, channels), part_of(xt, layer, channels)),
        None,
        lambda low: halved(last_weights, low),
        bias[layer],
        lambda at: cells[layer, at, :],
        memory,
        hidden,
        gate_rows,
        shifted,
    )
    copy.wait()


def pack_kernel(rows, first_own, second_own, first_got, second_got, packed, sent, next_edge, taps, cell_edge):
    channels = sent.shape[0]
    layers = cell_edge.shape[0]
    layer = layers - 1
    edge = 2 * rows
    even = tile_place() % 2 == 0
    own_right = jnp.where(even, first_own[...], second_own[...])
    own_left = jnp.where(even, second_own[...], first_own[...])
    from_left = jnp.where(even, second_got[...], first_got[...])
    from_right = jnp.where(even, first_got[...], second_got[...])
    from_left = jnp.where(tile_place() > 0, from_left, jnp.zeros_like(from_left))
    from_right = jnp.where(tile_place() < GRID_COLS - 1, from_right, jnp.zeros_like(from_right))
    lane = iota((channels, LANES), 1)

    def laid(k, pieces):
        out = jnp.zeros((channels, LANES), bf16)
        for slot, (value, block) in enumerate(pieces):
            value = turned(value, (slot - block) * rows - k * edge)
            out = jnp.where((lane >= slot * rows) & (lane < (slot + 1) * rows), value, out)
        return out

    outer = [(from_left, 0), (own_right, 1), (from_left, 1), (from_right, 1), (own_left, 1), (from_right, 0)]
    for k in range(layers + 1):
        packed[k] = laid(k, outer)
    sent[...] = packed[layer]
    next_edge[...] = laid(layers + 1, outer)
    inner = [
        [(from_left, 0), (own_right, 1), (from_left, 1), (own_right, 0)],
        [(from_left, 1), (from_right, 1), (own_left, 1), (own_right, 1)],
        [(own_left, 1), (from_right, 0), (own_left, 0), (from_right, 1)],
    ]
    for b in range(3):
        for k in range(2):
            taps[b, k * channels : (k + 1) * channels] = laid(layer - 1 + k, inner[b])
    for k in range(layers):
        high, low = (
            laid(layers + 2 + k, [(value, part) for value in (from_left, from_right, own_left, own_right)])
            for part in range(2)
        )
        cell_edge[k] = high.astype(f32) + low.astype(f32)


def mend_kernel(taps, last_weights, bias, cell_edge, hidden, last, edge_memory, edge_gates):
    rows, channels, _ = hidden.shape
    layer = bias.shape[0] - 1
    gates, memory, edge_hidden = edge_step(
        [taps[b] for b in range(3)], last_weights[...], bias[layer], cell_edge[layer], rows
    )
    last[rows] = outer_columns(edge_hidden, rows)
    for r in range(rows):
        last[r] = mended(hidden[r], edge_hidden, r, rows)
    edge_memory[...] = memory
    for q in range(4):
        edge_gates[q * channels : (q + 1) * channels] = gates[q].astype(bf16)


def halved(weights, low):
    channels = weights.shape[0] // 4
    parts = [weights[q * channels + low : q * channels + low + channels // 2] for q in range(4)]
    return jnp.concatenate(parts, axis=0)


def settle_kernel(rough_gates, rough_memory, edge_gates, edge_memory, last_memory, last_tiles, last_gates):
    rows, gate_count, _ = rough_gates.shape
    channels = gate_count // 4
    order = swap_matrix(rows, 256 // rows, False)
    for r in range(rows):
        last_gates[r] = mended(rough_gates[r], edge_gates[...], r, rows)
    for first in range(0, last_tiles.shape[0], 512):
        restore(order, last_gates, last_tiles, first)
    for r in range(rows):
        at = pl.ds(r, channels, stride=rows)
        last_memory[at, :] = mended(rough_memory[at, :], edge_memory[...], r, rows)


def middle_kernel(
    xt, packet, packet_edge, packed, first_weights, last_weights, bias, cells, cell_edge,
    last, last_memory, last_tiles,
    before, before_memory, next_gates, next_memory, next_hidden, gates,
    shifted, first_gates, tiles, sems, last_sem,
):
    first = lax.axis_index("section") == 0
    rows, channels, _ = packet.shape
    layers = bias.shape[0]
    order = swap_matrix(rows, 256 // rows, False)
    started = [pltpu.make_async_copy(last_tiles, gates.at[0, layers - 1], last_sem)]
    started[0].start()
    edges = (jnp.where(first, packed[layers], packet_edge[...]), packed[0])

    def outside():
        wide = jnp.concatenate(edges, axis=0)
        columns = [turned(wide, -2 * rows * b) for b in range(3)]
        _, _, hidden = edge_step(columns, first_weights[...], bias[0], cell_edge[0], rows)
        before[rows] = outer_columns(hidden, rows)

    run_layer(
        (either(first, part_of(xt, layers, channels), whole(packet)), part_of(xt, 0, channels)),
        edges,
        lambda low: halved(first_weights, low),
        bias[0],
        lambda at: cells[0, at, :],
        before_memory,
        before,
        first_gates,
        shifted,
    )
    outside()
    run_layer(
        (whole(before), whole(last)),
        (before[rows], last[rows]),
        last_weights[...],
        bias[layers - 1],
        lambda at: last_memory[at, :],
        next_memory,
        next_hidden,
        next_gates,
        shifted,
        dealt(saves(order, first_gates, tiles, gates.at[0, 0], sems, started), rows // 2),
    )
    for copy in started:
        copy.wait()


def final_kernel(
    xt, packet, next_edge, before, first_weights, bias, before_memory, last_gates, last_memory, last_hidden, _,
    gates, hidden_out, memory_out,
    shifted, first_gates, tiles, other_tiles, first_hidden, first_memory, hidden_tiles, other_hidden, sems, cell_sems,
):
    first = lax.axis_index("section") == 0
    rows = packet.shape[0] - 1
    channels = packet.shape[1]
    layer = bias.shape[0] - 1
    order = swap_matrix(rows, 256 // rows, False)
    started = [pltpu.make_async_copy(last_memory, memory_out.at[layer], cell_sems.at[0])]
    started[0].start()
    frame = xt.shape[1] // channels - 1
    for work in saves(order, last_gates, tiles, gates.at[1, layer], sems.at[0], started):
        work()
    for work in saves(order, last_hidden, hidden_tiles, hidden_out.at[layer], sems.at[2], started):
        work()
    run_layer(
        (either(first, part_of(xt, frame, channels), whole(packet)), whole(before)),
        (jnp.where(first, next_edge[...], packet[rows]), before[rows]),
        lambda low: halved(first_weights, low),
        bias[0],
        lambda at: before_memory[at, :],
        first_memory,
        first_hidden,
        first_gates,
        shifted,
    )
    copy = pltpu.make_async_copy(first_memory, memory_out.at[0], cell_sems.at[1])
    copy.start()
    started.append(copy)
    for work in saves(order, first_gates, other_tiles, gates.at[1, 0], sems.at[1], started):
        work()
    for work in saves(order, first_hidden, other_hidden, hidden_out.at[0], sems.at[3], started):
        work()
    for copy in started:
        copy.wait()


def wavefront(frames, hidden_init, memory_init, weights, biases):
    steps, _, channels, rows, _ = frames.shape
    layers, gate_count, depth = weights.shape
    flat = channels * rows
    frames = in_hbm(frames.reshape(steps, flat, LANES))
    hidden_init = in_hbm(hidden_init.reshape(layers, flat, LANES))
    memory_init = in_hbm(memory_init.reshape(layers, flat, LANES))
    weights, biases = in_hbm(weights), in_hbm(biases)
    plane = (channels, LANES)
    sections = lax.axis_size("section")
    ahead = [(i, (i + 1) % sections) for i in range(sections)]

    def call(kernel, ins, outs, scratch=(), hbm=(), out_specs=None, aliases=None):
        return pl.pallas_call(
            kernel,
            in_specs=[HBM if i in hbm else VMEM for i in range(len(ins))],
            out_specs=out_specs or [VMEM] * len(outs),
            out_shape=outs,
            scratch_shapes=list(scratch),
            input_output_aliases=aliases or {},
            compiler_params=params(),
        )(*ins)

    state = pltpu.VMEM((rows,) + plane, bf16)
    state_and_edge = pltpu.VMEM((rows + 1,) + plane, bf16)
    memory = pltpu.VMEM((flat, LANES), f32)
    edge = pltpu.VMEM(plane, bf16)
    layer_weights = pltpu.VMEM((gate_count, depth), bf16)
    gate_rows = pltpu.VMEM((rows, gate_count, LANES), bf16)
    shifted = pltpu.VMEM((3, rows + 2, 2 * channels, LANES), bf16)
    gate_tiles = pltpu.VMEM((gate_count * rows, LANES), bf16)
    hidden_tiles = pltpu.VMEM((flat, LANES), bf16)
    pieces = gate_count * rows // 512

    xt, sent, first_edges, second_edges, cells, wide_bias, last_weights = call(
        prep_kernel,
        (frames, hidden_init, memory_init, biases, weights),
        [
            pltpu.VMEM((rows, (layers + steps) * channels, LANES), bf16),
            state,
            edge,
            edge,
            pltpu.VMEM((layers, flat, LANES), f32),
            pltpu.VMEM((layers, gate_count, LANES), f32),
            layer_weights,
        ],
        [
            pltpu.VMEM((layers + steps, flat, LANES), bf16),
            pltpu.VMEM((layers, gate_count), f32),
            pltpu.SemaphoreType.DMA((5,)),
        ],
        hbm=range(5),
    )
    packet = permuted(sent, "section", ahead)
    first_got = permuted(first_edges, "tile", swap_pairs(0))
    second_got = permuted(second_edges, "tile", swap_pairs(1))
    rough_gates, rough_memory, rough_hidden, first_weights = call(
        first_last_layer,
        (xt, wide_bias, cells, weights, last_weights),
        [gate_rows, memory, state, layer_weights],
        [shifted, pltpu.SemaphoreType.DMA],
        hbm=(3,),
    )
    packed, sent_edge, next_edge, taps, cell_edge = call(
        functools.partial(pack_kernel, rows),
        (first_edges, second_edges, first_got, second_got),
        [
            pltpu.VMEM((layers + 1,) + plane, bf16),
            edge,
            edge,
            pltpu.VMEM((3, 2 * channels, LANES), bf16),
            pltpu.VMEM((layers,) + plane, f32),
        ],
    )
    packet_edge = permuted(sent_edge, "section", ahead)
    last, edge_memory, edge_gates = call(
        mend_kernel,
        (taps, last_weights, wide_bias, cell_edge, rough_hidden),
        [state_and_edge, pltpu.VMEM(plane, f32), pltpu.VMEM((gate_count, LANES), bf16)],
    )
    next_packet = permuted(last, "section", ahead)
    gates_shape = jax.ShapeDtypeStruct((steps, layers, gate_count * rows, LANES), bf16)
    last_memory, last_tiles = call(
        settle_kernel,
        (rough_gates, rough_memory, edge_gates, edge_memory),
        [memory, gate_tiles],
        [gate_rows],
    )
    before, before_memory, next_gates, next_memory, next_hidden, gates = call(
        middle_kernel,
        (
            xt, packet, packet_edge, packed, first_weights, last_weights, wide_bias, cells, cell_edge,
            last, last_memory, last_tiles,
        ),
        [state_and_edge, memory, gate_rows, memory, state, gates_shape],
        [shifted, gate_rows, gate_tiles, pltpu.SemaphoreType.DMA((pieces,)), pltpu.SemaphoreType.DMA],
        out_specs=[VMEM] * 5 + [HBM],
    )
    gates, hidden_out, memory_out = call(
        final_kernel,
        (
            xt, next_packet, next_edge, before, first_weights, wide_bias, before_memory,
            next_gates, next_memory, next_hidden, gates,
        ),
        [
            gates_shape,
            jax.ShapeDtypeStruct((layers, flat, LANES), bf16),
            jax.ShapeDtypeStruct((layers, flat, LANES), f32),
        ],
        [
            shifted, gate_rows, gate_tiles, gate_tiles, state, memory, hidden_tiles, hidden_tiles,
            pltpu.SemaphoreType.DMA((4, pieces)), pltpu.SemaphoreType.DMA((2,)),
        ],
        hbm=(10,),
        out_specs=[HBM] * 3,
        aliases={10: 0},
    )
    return (
        hidden_out.reshape(layers, 1, channels, rows, LANES),
        memory_out.reshape(layers, 1, channels, rows, LANES),
        gates.reshape(steps, layers, 1, gate_count, rows, LANES),
    )


def from_behind(block, axis, distance):
    devices = range(lax.axis_size(axis))
    route = [((i - distance) % len(devices), i) for i in devices]
    return lax.ppermute(block, axis, route)


def shifted(shard, axis, by):
    peers = lax.axis_size(axis)
    pairs = [(i, i + by) for i in range(peers) if 0 <= i + by < peers]
    return lax.ppermute(shard, axis, pairs)


def keep_if(condition, rim):
    return jnp.where(condition, rim, jnp.zeros_like(rim))


def with_rims(source_field):
    place = tile_place()
    row_place, column_place = (place // GRID_COLS, place % GRID_COLS)
    grid_rows = lax.axis_size("tile") // GRID_COLS
    upper_rim = from_behind(source_field[:, -1:, :], "tile", GRID_COLS)
    lower_rim = from_behind(source_field[:, :1, :], "tile", -GRID_COLS)
    upper_rim = keep_if(row_place > 0, upper_rim)
    lower_rim = keep_if(row_place < grid_rows - 1, lower_rim)
    heightened = jnp.concatenate([upper_rim, source_field, lower_rim], axis=1)
    left_rim = from_behind(heightened[:, :, -1:], "tile", 1)
    right_rim = from_behind(heightened[:, :, :1], "tile", -1)
    left_rim = keep_if(column_place > 0, left_rim)
    right_rim = keep_if(column_place < GRID_COLS - 1, right_rim)
    return jnp.concatenate([left_rim, heightened, right_rim], axis=2)


def hand_over(hidden_state):
    return shifted(hidden_state, "section", 1)


def advance(stacked, layer_weights, bias_row, memory):
    hidden_count = memory.shape[0]
    height = stacked.shape[1] - 2
    breadth = stacked.shape[2] - 2
    shifted_views = [
        stacked[:, row_offset : row_offset + height, column_offset : column_offset + breadth]
        for row_offset in range(3)
        for column_offset in range(3)
    ]
    patches = jnp.concatenate(shifted_views, axis=0).reshape(9 * stacked.shape[0], height * breadth)
    preact = jnp.dot(layer_weights, patches, preferred_element_type=jnp.float32) + bias_row[:, None]
    preact = preact.reshape(4, hidden_count, height, breadth)
    inflow = jax.nn.sigmoid(preact[0])
    forget = jax.nn.sigmoid(preact[1])
    outflow = jax.nn.sigmoid(preact[2])
    candidate = jnp.tanh(preact[3])
    memory = forget * memory + inflow * candidate
    hidden_state = (outflow * jnp.tanh(memory)).astype(jnp.bfloat16)
    opened = (
        jnp.stack([inflow, forget, outflow, candidate])
        .reshape(4 * hidden_count, height, breadth)
        .astype(jnp.bfloat16)
    )
    return (hidden_state, memory, opened)


def general_body(frames, hidden_init, memory_init, weights, biases):
    step_count = frames.shape[0]
    layer_count = weights.shape[0]
    channels = frames.shape[2]
    first_section = lax.axis_index("section") == 0
    saved_gates = []
    states = [hidden_init[layer_index, 0] for layer_index in range(layer_count)]
    memories = [memory_init[layer_index, 0] for layer_index in range(layer_count)]
    for moment in range(step_count):
        received = hand_over(states[-1])
        incoming = jnp.where(first_section, frames[moment, 0], received)
        padded = with_rims(jnp.concatenate([incoming] + states, axis=0))
        layer_stacks = [
            padded[layer_index * channels : (layer_index + 2) * channels]
            for layer_index in range(layer_count)
        ]
        fresh_states = []
        fresh_memories = []
        opened_step = []
        for layer_index in range(layer_count):
            hidden_state, memory, opened = advance(
                layer_stacks[layer_index],
                weights[layer_index],
                biases[layer_index],
                memories[layer_index],
            )
            fresh_states.append(hidden_state)
            fresh_memories.append(memory)
            opened_step.append(opened)
        states = fresh_states
        memories = fresh_memories
        saved_gates.append(jnp.stack(opened_step))
    hidden_out = jnp.stack(states)[:, None]
    memory_out = jnp.stack(memories)[:, None]
    gates_out = jnp.stack(saved_gates)[:, :, None]
    return (hidden_out, memory_out, gates_out)


def body(frames, hidden_init, memory_init, weights, biases):
    one_row = lax.axis_size("tile") == GRID_COLS
    if one_row and frames.shape[0] == 2 and weights.shape[0] == 2:
        return wavefront(frames, hidden_init, memory_init, weights, biases)
    return general_body(frames, hidden_init, memory_init, weights, biases)


def solution(mesh):
    in_specs = (
        P(None, ("member", "tile"), None, None, None),
        P("section", ("member", "tile"), None, None, None),
        P("section", ("member", "tile"), None, None, None),
        P("section", None, None),
        P("section", None),
    )
    out_specs = (
        P("section", ("member", "tile"), None, None, None),
        P("section", ("member", "tile"), None, None, None),
        P(None, "section", ("member", "tile"), None, None, None),
    )
    return jax.shard_map(body, mesh=mesh, in_specs=in_specs, out_specs=out_specs, check_vma=False)
```

```python
import functools

import jax
import jax.numpy as jnp
from jax import lax
from jax.experimental import pallas as pl
from jax.experimental.pallas import tpu as pltpu
from jax.sharding import PartitionSpec as P


GRID_COLS = 8
LANES = 128

bf16 = jnp.bfloat16
f32 = jnp.float32
VMEM = pl.BlockSpec(memory_space=pltpu.VMEM)
HBM = pl.BlockSpec(memory_space=pltpu.HBM)


def iota(shape, dim):
    return lax.broadcasted_iota(jnp.int32, shape, dim)


def params():
    return pltpu.CompilerParams(vmem_limit_bytes=24 * 2**20)


def in_vmem(array):
    return pltpu.with_memory_space_constraint(array, pltpu.VMEM)


def in_hbm(array):
    return pltpu.with_memory_space_constraint(array, pltpu.HBM)


def permuted(array, axis, pairs):
    return in_vmem(lax.ppermute(array, axis, pairs))


def tile_place():
    return (lax.axis_index("tile") + GRID_COLS + GRID_COLS // 2) % lax.axis_size("tile")


def swap_pairs(parity):
    count = lax.axis_size("tile")
    index = {(k + GRID_COLS + GRID_COLS // 2) % count: k for k in range(count)}
    pairs = []
    for place in range(parity, count, 2):
        one, other = index[place], index[(place + 1) % count]
        pairs += [(one, other), (other, one)]
    return pairs


def halves(value, base):
    return (value >> (base.bit_length() - 1), value & (base - 1))


def swap_matrix(rows, block, to_rows_first):
    size = rows * block
    m = iota((size, size), 0)
    n = iota((size, size), 1)
    if to_rows_first:
        m, n = n, m
    channel, row = halves(m, rows)
    other_row, other_channel = halves(n, block)
    return jnp.where((channel == other_channel) & (row == other_row), 1.0, 0.0).astype(bf16)


def turned(value, by):
    return pltpu.roll(value, by % LANES, 1)


def prep_kernel(
    frames, hidden, memory, bias, weights, xt, sent, first_edges, second_edges, cells, wide_bias, last_weights,
    raw, raw_bias, sems,
):
    layers, _, _ = hidden.shape
    rows, channels, _ = sent.shape
    copies = [
        pltpu.make_async_copy(hidden, raw.at[pl.ds(0, layers)], sems.at[0]),
        pltpu.make_async_copy(frames, raw.at[pl.ds(layers, frames.shape[0])], sems.at[1]),
        pltpu.make_async_copy(memory, cells, sems.at[2]),
        pltpu.make_async_copy(bias, raw_bias, sems.at[3]),
    ]
    copies.append(pltpu.make_async_copy(weights.at[layers - 1], last_weights, sems.at[4]))
    copies[3].start()
    for copy in copies[:3] + copies[4:]:
        copy.start()
    copies[3].wait()
    blocks = [raw_bias[k : k + 1, q * channels : (q + 1) * channels] for k in range(layers) for q in range(4)]
    columns = jnp.concatenate(blocks + [jnp.zeros((channels - len(blocks), channels), f32)], axis=0).T
    for k in range(layers):
        for q in range(4):
            part = jnp.broadcast_to(columns[:, 4 * k + q : 4 * k + q + 1], (channels, LANES))
            wide_bias[k, q * channels : (q + 1) * channels] = part * (0.5 if q < 3 else 1.0)

    block = 256 // rows
    order = swap_matrix(rows, block, True)
    count = raw.shape[0]
    width = rows * LANES
    m = iota((width, LANES), 0)
    lane = iota((width, LANES), 1)
    near, row = halves(lane, rows)
    to_right = (lane < 2 * rows) & (m == row * LANES + (LANES - 2) + near)
    to_left = (lane < 2 * rows) & (m == row * LANES + 1 - near)
    select = jnp.concatenate(
        [jnp.where(to_right, 1.0, 0.0).astype(bf16), jnp.where(to_left, 1.0, 0.0).astype(bf16)], axis=1
    )
    for pair in range(0, count, 2):
        copies[pair // layers].wait()
        for group in range(channels // block):
            part = pl.ds(group * 256, 256)
            both = jnp.concatenate([raw[pair, part], raw[pair + 1, part]], axis=1)
            out = jnp.dot(order, both, preferred_element_type=f32).astype(bf16)
            for r in range(rows):
                for k in range(2):
                    piece = out[r * block : (r + 1) * block, k * LANES : (k + 1) * LANES]
                    at = (pair + k) * channels + group * block
                    xt[r, at : at + block] = piece
                    if pair + k == layers - 1:
                        sent[r, group * block : (group + 1) * block] = piece
    edge = 2 * rows
    m = iota((2 * LANES, 2 * LANES), 0)
    part, place = halves(m, LANES)
    layer_of, place = halves(place, edge)
    row, side = halves(place, 2)
    target = side * LANES + (count + layer_of) * edge + part * rows + row
    spread = (layer_of < layers) & (iota((2 * LANES, 2 * LANES), 1) == target)
    spread = jnp.where(spread, 1.0, 0.0).astype(bf16)
    copies[2].wait()
    lane_pair = iota((channels, LANES), 1) >> 1
    cell_columns = jnp.zeros((channels, LANES), f32)
    for layer in range(layers):
        for r in range(rows):
            moved = turned(cells[layer, pl.ds(r, channels, stride=rows), :], layer * edge + 2 * r + 1)
            cell_columns = jnp.where(lane_pair == layer * rows + r, moved, cell_columns)
    high = cell_columns.astype(bf16)
    low = (cell_columns - high.astype(f32)).astype(bf16)
    wide = jnp.concatenate([xt[r] for r in range(rows)], axis=1)
    edges = jnp.dot(wide, select, preferred_element_type=f32)
    out = jnp.dot(jnp.concatenate([high, low], axis=1), spread, preferred_element_type=f32)
    right, left = out[:, :LANES], out[:, LANES:]
    for k in range(count):
        part = edges[k * channels : (k + 1) * channels]
        right += turned(part[:, :LANES], k * edge)
        left += turned(part[:, LANES:], k * edge)
    even = tile_place() % 2 == 0
    first_edges[...] = jnp.where(even, right, left).astype(bf16)
    second_edges[...] = jnp.where(even, left, right).astype(bf16)
    copies[4].wait()


def cell_step(pre, bias, memory):
    channels = memory.shape[0]

    def gate(q):
        part = slice(q * channels, (q + 1) * channels)
        if q == 3:
            return jnp.tanh(pre[part] + bias[part])
        return jnp.tanh(pre[part] * 0.5 + bias[part]) * 0.5 + 0.5

    inflow, forget, outflow, candidate = gate(0), gate(1), gate(2), gate(3)
    memory = forget * memory + inflow * candidate
    hidden = (outflow * jnp.tanh(memory)).astype(bf16)
    return (inflow, forget, outflow, candidate), memory, hidden


def run_layer(sources, edge_columns, weights, bias, memory_of, memory_out, hidden_rows, gate_rows, shifted, beside=()):
    rows = shifted.shape[1] - 2
    channels = shifted.shape[2] // 2
    lane = iota((channels, LANES), 1)
    blank = jnp.zeros((2 * channels, LANES), bf16)
    for b in range(3):
        shifted[b, 0] = blank
        shifted[b, rows + 1] = blank

    def build(r):
        for k in range(2):
            part = slice(k * channels, (k + 1) * channels)
            x = sources[k](r)
            if edge_columns is None:
                before = after = jnp.zeros_like(x)
            else:
                before = turned(edge_columns[k], -2 * rows - r)
                after = turned(edge_columns[k], -1 - 3 * rows - r)
            shifted[1, r + 1, part] = x
            shifted[0, r + 1, part] = jnp.where(lane == 0, before, turned(x, 1))
            shifted[2, r + 1, part] = jnp.where(lane == LANES - 1, after, turned(x, -1))

    for r in range(rows):
        build(r)
    tiles = rows // 2
    parts = 1 if beside else 2
    size = channels // parts
    for low in range(0, channels, size):
        chosen = [slice(q * channels + low, q * channels + low + size) for q in range(4)]
        if parts == 1:
            part_weights, part_bias = weights, bias
        else:
            part_weights = weights(low)
            part_bias = jnp.concatenate([bias[c] for c in chosen], axis=0)
        for j in range(tiles):
            for work in beside[j] if beside else ():
                work()
            patches = jnp.concatenate(
                [
                    jnp.concatenate([shifted[b, 2 * j + a], shifted[b, 2 * j + a + 1]], axis=1)
                    for a in range(3)
                    for b in range(3)
                ],
                axis=0,
            )
            total = jnp.dot(part_weights, patches, preferred_element_type=f32)
            for k in range(2):
                r = 2 * j + k
                at = pl.ds(r + rows * low, size, stride=rows)
                gates, memory, hidden = cell_step(total[:, k * LANES : (k + 1) * LANES], part_bias, memory_of(at))
                memory_out[at, :] = memory
                hidden_rows[r, low : low + size] = hidden
                for q in range(4):
                    gate_rows[r, chosen[q]] = gates[q].astype(bf16)


def edge_step(columns, weights, bias, memory, rows):
    channels = memory.shape[0]
    lane = iota((2 * channels, LANES), 1)
    parts = []
    pixel_row = lane & (rows - 1)
    for a in range(3):
        row = pixel_row + (a - 1)
        for b in range(3):
            moved = turned(columns[b], 1 - a)
            parts.append(jnp.where((row >= 0) & (row < rows), moved, jnp.zeros_like(moved)))
    total = jnp.dot(weights, jnp.concatenate(parts, axis=0), preferred_element_type=f32)
    return cell_step(total, bias, memory)


def outer_columns(hidden, rows):
    lane = iota(hidden.shape, 1)
    place = tile_place() % GRID_COLS
    inside = ((lane < rows) & (place > 0)) | ((lane >= rows) & (lane < 2 * rows) & (place < GRID_COLS - 1))
    return turned(jnp.where(inside, hidden, jnp.zeros_like(hidden)), 2 * rows)


def restore(order, source, target, first):
    rows = source.shape[0]
    block = 256 // rows
    both = []
    for at in (first // rows, first // rows + block):
        both.append(jnp.concatenate([source[r, at : at + block] for r in range(rows)], axis=0))
    out = jnp.dot(order, jnp.concatenate(both, axis=1), preferred_element_type=f32).astype(bf16)
    target[first : first + 256] = out[:, :LANES]
    target[first + 256 : first + 512] = out[:, LANES:]


def saves(order, source, tiles, out, sems, started):
    def piece(first):
        def work():
            restore(order, source, tiles, first)
            part = pl.ds(first, 512)
            copy = pltpu.make_async_copy(tiles.at[part], out.at[part], sems.at[first // 512])
            copy.start()
            started.append(copy)

        return work

    return [piece(first) for first in range(0, tiles.shape[0], 512)]


def dealt(works, hands):
    share = -(-len(works) // hands)
    return [works[j * share : (j + 1) * share] for j in range(hands)]


def mended(value, column, r, rows):
    lane = iota(value.shape, 1)
    value = jnp.where(lane == 0, turned(column, -2 * rows - r), value)
    return jnp.where(lane == LANES - 1, turned(column, -1 - 3 * rows - r), value)


def part_of(ref, k, channels):
    def load(r):
        return ref[r, k * channels : (k + 1) * channels]

    return load


def either(condition, one, other):
    def load(r):
        return jnp.where(condition, one(r), other(r))

    return load


def whole(ref):
    return lambda r: ref[r]


def first_last_layer(xt, bias, cells, weights, last_weights, gate_rows, memory, hidden, first_weights, shifted, sem):
    layer = bias.shape[0] - 1
    channels = hidden.shape[1]
    copy = pltpu.make_async_copy(weights.at[0], first_weights, sem)
    copy.start()
    run_layer(
        (part_of(xt, layer - 1, channels), part_of(xt, layer, channels)),
        None,
        lambda low: halved(last_weights, low),
        bias[layer],
        lambda at: cells[layer, at, :],
        memory,
        hidden,
        gate_rows,
        shifted,
    )
    copy.wait()


def pack_kernel(rows, first_own, second_own, first_got, second_got, packed, sent, next_edge, taps, cell_edge):
    channels = sent.shape[0]
    layers = cell_edge.shape[0]
    layer = layers - 1
    edge = 2 * rows
    even = tile_place() % 2 == 0
    own_right = jnp.where(even, first_own[...], second_own[...])
    own_left = jnp.where(even, second_own[...], first_own[...])
    from_left = jnp.where(even, second_got[...], first_got[...])
    from_right = jnp.where(even, first_got[...], second_got[...])
    from_left = jnp.where(tile_place() > 0, from_left, jnp.zeros_like(from_left))
    from_right = jnp.where(tile_place() < GRID_COLS - 1, from_right, jnp.zeros_like(from_right))
    lane = iota((channels, LANES), 1)

    def laid(k, pieces):
        out = jnp.zeros((channels, LANES), bf16)
        for slot, (value, block) in enumerate(pieces):
            value = turned(value, (slot - block) * rows - k * edge)
            out = jnp.where((lane >= slot * rows) & (lane < (slot + 1) * rows), value, out)
        return out

    outer = [(from_left, 0), (own_right, 1), (from_left, 1), (from_right, 1), (own_left, 1), (from_right, 0)]
    for k in range(layers + 1):
        packed[k] = laid(k, outer)
    sent[...] = packed[layer]
    next_edge[...] = laid(layers + 1, outer)
    inner = [
        [(from_left, 0), (own_right, 1), (from_left, 1), (own_right, 0)],
        [(from_left, 1), (from_right, 1), (own_left, 1), (own_right, 1)],
        [(own_left, 1), (from_right, 0), (own_left, 0), (from_right, 1)],
    ]
    for b in range(3):
        for k in range(2):
            taps[b, k * channels : (k + 1) * channels] = laid(layer - 1 + k, inner[b])
    for k in range(layers):
        high, low = (
            laid(layers + 2 + k, [(value, part) for value in (from_left, from_right, own_left, own_right)])
            for part in range(2)
        )
        cell_edge[k] = high.astype(f32) + low.astype(f32)


def mend_kernel(taps, last_weights, bias, cell_edge, hidden, last, edge_memory, edge_gates):
    rows, channels, _ = hidden.shape
    layer = bias.shape[0] - 1
    gates, memory, edge_hidden = edge_step(
        [taps[b] for b in range(3)], last_weights[...], bias[layer], cell_edge[layer], rows
    )
    last[rows] = outer_columns(edge_hidden, rows)
    for r in range(rows):
        last[r] = mended(hidden[r], edge_hidden, r, rows)
    edge_memory[...] = memory
    for q in range(4):
        edge_gates[q * channels : (q + 1) * channels] = gates[q].astype(bf16)


def halved(weights, low):
    channels = weights.shape[0] // 4
    parts = [weights[q * channels + low : q * channels + low + channels // 2] for q in range(4)]
    return jnp.concatenate(parts, axis=0)


def settle_kernel(rough_gates, rough_memory, edge_gates, edge_memory, last_memory, last_tiles, last_gates):
    rows, gate_count, _ = rough_gates.shape
    channels = gate_count // 4
    order = swap_matrix(rows, 256 // rows, False)
    for r in range(rows):
        last_gates[r] = mended(rough_gates[r], edge_gates[...], r, rows)
    for first in range(0, last_tiles.shape[0], 512):
        restore(order, last_gates, last_tiles, first)
    for r in range(rows):
        at = pl.ds(r, channels, stride=rows)
        last_memory[at, :] = mended(rough_memory[at, :], edge_memory[...], r, rows)


def middle_kernel(
    xt, packet, packet_edge, packed, first_weights, last_weights, bias, cells, cell_edge,
    last, last_memory, last_tiles,
    before, before_memory, next_gates, next_memory, next_hidden, gates,
    shifted, first_gates, tiles, sems, last_sem,
):
    first = lax.axis_index("section") == 0
    rows, channels, _ = packet.shape
    layers = bias.shape[0]
    order = swap_matrix(rows, 256 // rows, False)
    started = [pltpu.make_async_copy(last_tiles, gates.at[0, layers - 1], last_sem)]
    started[0].start()
    edges = (jnp.where(first, packed[layers], packet_edge[...]), packed[0])

    def outside():
        wide = jnp.concatenate(edges, axis=0)
        columns = [turned(wide, -2 * rows * b) for b in range(3)]
        _, _, hidden = edge_step(columns, first_weights[...], bias[0], cell_edge[0], rows)
        before[rows] = outer_columns(hidden, rows)

    run_layer(
        (either(first, part_of(xt, layers, channels), whole(packet)), part_of(xt, 0, channels)),
        edges,
        lambda low: halved(first_weights, low),
        bias[0],
        lambda at: cells[0, at, :],
        before_memory,
        before,
        first_gates,
        shifted,
    )
    outside()
    run_layer(
        (whole(before), whole(last)),
        (before[rows], last[rows]),
        last_weights[...],
        bias[layers - 1],
        lambda at: last_memory[at, :],
        next_memory,
        next_hidden,
        next_gates,
        shifted,
        dealt(saves(order, first_gates, tiles, gates.at[0, 0], sems, started), rows // 2),
    )
    for copy in started:
        copy.wait()


def final_kernel(
    xt, packet, next_edge, before, first_weights, bias, before_memory, last_gates, last_memory, last_hidden, _,
    gates, hidden_out, memory_out,
    shifted, first_gates, tiles, other_tiles, first_hidden, first_memory, hidden_tiles, other_hidden, sems, cell_sems,
):
    first = lax.axis_index("section") == 0
    rows = packet.shape[0] - 1
    channels = packet.shape[1]
    layer = bias.shape[0] - 1
    order = swap_matrix(rows, 256 // rows, False)
    started = [pltpu.make_async_copy(last_memory, memory_out.at[layer], cell_sems.at[0])]
    started[0].start()
    frame = xt.shape[1] // channels - 1
    run_layer(
        (either(first, part_of(xt, frame, channels), whole(packet)), whole(before)),
        (jnp.where(first, next_edge[...], packet[rows]), before[rows]),
        first_weights[...],
        bias[0],
        lambda at: before_memory[at, :],
        first_memory,
        first_hidden,
        first_gates,
        shifted,
        dealt(
            saves(order, last_gates, tiles, gates.at[1, layer], sems.at[0], started)
            + saves(order, last_hidden, hidden_tiles, hidden_out.at[layer], sems.at[2], started),
            rows // 2,
        ),
    )
    copy = pltpu.make_async_copy(first_memory, memory_out.at[0], cell_sems.at[1])
    copy.start()
    started.append(copy)
    for work in saves(order, first_hidden, other_hidden, hidden_out.at[0], sems.at[3], started):
        work()
    for work in saves(order, first_gates, other_tiles, gates.at[1, 0], sems.at[1], started):
        work()
    for copy in started:
        copy.wait()


def wavefront(frames, hidden_init, memory_init, weights, biases):
    steps, _, channels, rows, _ = frames.shape
    layers, gate_count, depth = weights.shape
    flat = channels * rows
    frames = in_hbm(frames.reshape(steps, flat, LANES))
    hidden_init = in_hbm(hidden_init.reshape(layers, flat, LANES))
    memory_init = in_hbm(memory_init.reshape(layers, flat, LANES))
    weights, biases = in_hbm(weights), in_hbm(biases)
    plane = (channels, LANES)
    sections = lax.axis_size("section")
    ahead = [(i, (i + 1) % sections) for i in range(sections)]

    def call(kernel, ins, outs, scratch=(), hbm=(), out_specs=None, aliases=None):
        return pl.pallas_call(
            kernel,
            in_specs=[HBM if i in hbm else VMEM for i in range(len(ins))],
            out_specs=out_specs or [VMEM] * len(outs),
            out_shape=outs,
            scratch_shapes=list(scratch),
            input_output_aliases=aliases or {},
            compiler_params=params(),
        )(*ins)

    state = pltpu.VMEM((rows,) + plane, bf16)
    state_and_edge = pltpu.VMEM((rows + 1,) + plane, bf16)
    memory = pltpu.VMEM((flat, LANES), f32)
    edge = pltpu.VMEM(plane, bf16)
    layer_weights = pltpu.VMEM((gate_count, depth), bf16)
    gate_rows = pltpu.VMEM((rows, gate_count, LANES), bf16)
    shifted = pltpu.VMEM((3, rows + 2, 2 * channels, LANES), bf16)
    gate_tiles = pltpu.VMEM((gate_count * rows, LANES), bf16)
    hidden_tiles = pltpu.VMEM((flat, LANES), bf16)
    pieces = gate_count * rows // 512

    xt, sent, first_edges, second_edges, cells, wide_bias, last_weights = call(
        prep_kernel,
        (frames, hidden_init, memory_init, biases, weights),
        [
            pltpu.VMEM((rows, (layers + steps) * channels, LANES), bf16),
            state,
            edge,
            edge,
            pltpu.VMEM((layers, flat, LANES), f32),
            pltpu.VMEM((layers, gate_count, LANES), f32),
            layer_weights,
        ],
        [
            pltpu.VMEM((layers + steps, flat, LANES), bf16),
            pltpu.VMEM((layers, gate_count), f32),
            pltpu.SemaphoreType.DMA((5,)),
        ],
        hbm=range(5),
    )
    packet = permuted(sent, "section", ahead)
    first_got = permuted(first_edges, "tile", swap_pairs(0))
    second_got = permuted(second_edges, "tile", swap_pairs(1))
    rough_gates, rough_memory, rough_hidden, first_weights = call(
        first_last_layer,
        (xt, wide_bias, cells, weights, last_weights),
        [gate_rows, memory, state, layer_weights],
        [shifted, pltpu.SemaphoreType.DMA],
        hbm=(3,),
    )
    packed, sent_edge, next_edge, taps, cell_edge = call(
        functools.partial(pack_kernel, rows),
        (first_edges, second_edges, first_got, second_got),
        [
            pltpu.VMEM((layers + 1,) + plane, bf16),
            edge,
            edge,
            pltpu.VMEM((3, 2 * channels, LANES), bf16),
            pltpu.VMEM((layers,) + plane, f32),
        ],
    )
    packet_edge = permuted(sent_edge, "section", ahead)
    last, edge_memory, edge_gates = call(
        mend_kernel,
        (taps, last_weights, wide_bias, cell_edge, rough_hidden),
        [state_and_edge, pltpu.VMEM(plane, f32), pltpu.VMEM((gate_count, LANES), bf16)],
    )
    next_packet = permuted(last, "section", ahead)
    gates_shape = jax.ShapeDtypeStruct((steps, layers, gate_count * rows, LANES), bf16)
    last_memory, last_tiles = call(
        settle_kernel,
        (rough_gates, rough_memory, edge_gates, edge_memory),
        [memory, gate_tiles],
        [gate_rows],
    )
    before, before_memory, next_gates, next_memory, next_hidden, gates = call(
        middle_kernel,
        (
            xt, packet, packet_edge, packed, first_weights, last_weights, wide_bias, cells, cell_edge,
            last, last_memory, last_tiles,
        ),
        [state_and_edge, memory, gate_rows, memory, state, gates_shape],
        [shifted, gate_rows, gate_tiles, pltpu.SemaphoreType.DMA((pieces,)), pltpu.SemaphoreType.DMA],
        out_specs=[VMEM] * 5 + [HBM],
    )
    gates, hidden_out, memory_out = call(
        final_kernel,
        (
            xt, next_packet, next_edge, before, first_weights, wide_bias, before_memory,
            next_gates, next_memory, next_hidden, gates,
        ),
        [
            gates_shape,
            jax.ShapeDtypeStruct((layers, flat, LANES), bf16),
            jax.ShapeDtypeStruct((layers, flat, LANES), f32),
        ],
        [
            shifted, gate_rows, gate_tiles, gate_tiles, state, memory, hidden_tiles, hidden_tiles,
            pltpu.SemaphoreType.DMA((4, pieces)), pltpu.SemaphoreType.DMA((2,)),
        ],
        hbm=(10,),
        out_specs=[HBM] * 3,
        aliases={10: 0},
    )
    return (
        hidden_out.reshape(layers, 1, channels, rows, LANES),
        memory_out.reshape(layers, 1, channels, rows, LANES),
        gates.reshape(steps, layers, 1, gate_count, rows, LANES),
    )


def from_behind(block, axis, distance):
    devices = range(lax.axis_size(axis))
    route = [((i - distance) % len(devices), i) for i in devices]
    return lax.ppermute(block, axis, route)


def shifted(shard, axis, by):
    peers = lax.axis_size(axis)
    pairs = [(i, i + by) for i in range(peers) if 0 <= i + by < peers]
    return lax.ppermute(shard, axis, pairs)


def keep_if(condition, rim):
    return jnp.where(condition, rim, jnp.zeros_like(rim))


def with_rims(source_field):
    place = tile_place()
    row_place, column_place = (place // GRID_COLS, place % GRID_COLS)
    grid_rows = lax.axis_size("tile") // GRID_COLS
    upper_rim = from_behind(source_field[:, -1:, :], "tile", GRID_COLS)
    lower_rim = from_behind(source_field[:, :1, :], "tile", -GRID_COLS)
    upper_rim = keep_if(row_place > 0, upper_rim)
    lower_rim = keep_if(row_place < grid_rows - 1, lower_rim)
    heightened = jnp.concatenate([upper_rim, source_field, lower_rim], axis=1)
    left_rim = from_behind(heightened[:, :, -1:], "tile", 1)
    right_rim = from_behind(heightened[:, :, :1], "tile", -1)
    left_rim = keep_if(column_place > 0, left_rim)
    right_rim = keep_if(column_place < GRID_COLS - 1, right_rim)
    return jnp.concatenate([left_rim, heightened, right_rim], axis=2)


def hand_over(hidden_state):
    return shifted(hidden_state, "section", 1)


def advance(stacked, layer_weights, bias_row, memory):
    hidden_count = memory.shape[0]
    height = stacked.shape[1] - 2
    breadth = stacked.shape[2] - 2
    shifted_views = [
        stacked[:, row_offset : row_offset + height, column_offset : column_offset + breadth]
        for row_offset in range(3)
        for column_offset in range(3)
    ]
    patches = jnp.concatenate(shifted_views, axis=0).reshape(9 * stacked.shape[0], height * breadth)
    preact = jnp.dot(layer_weights, patches, preferred_element_type=jnp.float32) + bias_row[:, None]
    preact = preact.reshape(4, hidden_count, height, breadth)
    inflow = jax.nn.sigmoid(preact[0])
    forget = jax.nn.sigmoid(preact[1])
    outflow = jax.nn.sigmoid(preact[2])
    candidate = jnp.tanh(preact[3])
    memory = forget * memory + inflow * candidate
    hidden_state = (outflow * jnp.tanh(memory)).astype(jnp.bfloat16)
    opened = (
        jnp.stack([inflow, forget, outflow, candidate])
        .reshape(4 * hidden_count, height, breadth)
        .astype(jnp.bfloat16)
    )
    return (hidden_state, memory, opened)


def general_body(frames, hidden_init, memory_init, weights, biases):
    step_count = frames.shape[0]
    layer_count = weights.shape[0]
    channels = frames.shape[2]
    first_section = lax.axis_index("section") == 0
    saved_gates = []
    states = [hidden_init[layer_index, 0] for layer_index in range(layer_count)]
    memories = [memory_init[layer_index, 0] for layer_index in range(layer_count)]
    for moment in range(step_count):
        received = hand_over(states[-1])
        incoming = jnp.where(first_section, frames[moment, 0], received)
        padded = with_rims(jnp.concatenate([incoming] + states, axis=0))
        layer_stacks = [
            padded[layer_index * channels : (layer_index + 2) * channels]
            for layer_index in range(layer_count)
        ]
        fresh_states = []
        fresh_memories = []
        opened_step = []
        for layer_index in range(layer_count):
            hidden_state, memory, opened = advance(
                layer_stacks[layer_index],
                weights[layer_index],
                biases[layer_index],
                memories[layer_index],
            )
            fresh_states.append(hidden_state)
            fresh_memories.append(memory)
            opened_step.append(opened)
        states = fresh_states
        memories = fresh_memories
        saved_gates.append(jnp.stack(opened_step))
    hidden_out = jnp.stack(states)[:, None]
    memory_out = jnp.stack(memories)[:, None]
    gates_out = jnp.stack(saved_gates)[:, :, None]
    return (hidden_out, memory_out, gates_out)


def body(frames, hidden_init, memory_init, weights, biases):
    one_row = lax.axis_size("tile") == GRID_COLS
    if one_row and frames.shape[0] == 2 and weights.shape[0] == 2:
        return wavefront(frames, hidden_init, memory_init, weights, biases)
    return general_body(frames, hidden_init, memory_init, weights, biases)


def solution(mesh):
    in_specs = (
        P(None, ("member", "tile"), None, None, None),
        P("section", ("member", "tile"), None, None, None),
        P("section", ("member", "tile"), None, None, None),
        P("section", None, None),
        P("section", None),
    )
    out_specs = (
        P("section", ("member", "tile"), None, None, None),
        P("section", ("member", "tile"), None, None, None),
        P(None, "section", ("member", "tile"), None, None, None),
    )
    return jax.shard_map(body, mesh=mesh, in_specs=in_specs, out_specs=out_specs, check_vma=False)
```
